256 devices in a mesh: walk: 16 (over z, x_hi), blk: 16 (over x_lo, y, core).
Axes of the slice: x: 4 (x_hi: 2, x_lo: 2; x = x_hi * 2 + x_lo), y: 4, z: 8, core: 2. Of those that a mesh axis runs over, the one named last changes fastest.
Arguments:
- vertex_times: int32 [16, 1024], P('blk'), may hold values from 0 to 4095
- vertex_sites: int32 [16, 1024], P('blk'), may hold values from 0 to 15
- vertex_matrix: bfloat16 [16, 1024, 1024], P('blk', 'walk'), may hold values from -0.1875 to 0.1875
- bare_green: float32 [2, 1024], replicated, may hold values from -3 to 3
- transfer_momentum: int32 [16], replicated, may hold values from 0 to 15, each once
- transfers: int32 [32], replicated, may hold values from 0 to 31, each once
Outputs:
- g4: float32 [2, 32, 1024, 1024], P(None, 'blk', 'walk')
The draws below stay inside these ranges and needn't reach their ends.
Inputs may be any that keep to these rules, and one draw needn't show every extreme that they name: `transfer_momentum`: each of 0 to 15 appears exactly once. `transfers`: each of 0 to 31 appears exactly once.
All inputs are finite; a program needn't handle non-finite values.
Results may differ from the reference program's by a relative error of at most 0.0071.
Values may be sent and summed in bfloat16 or wider, within the bound.
A program may use at most 64 MiB of HBM per device.

```python
import math
import jax
import jax.numpy as jnp
from jax import lax

NM = 16
NF = 64
NV = 1024
NT = 4096
KS = 1024
NW = 16
NQ = 32


def plant(values, key, smallest, largest):
    dims = values.shape
    place = [jax.random.randint(jax.random.fold_in(key, axis), (), 0, dims[axis]) for axis in range(len(dims))]
    values = values.at[tuple(place)].set(smallest)
    longest = dims.index(max(dims))
    place[longest] = (place[longest] + 1) % dims[longest]
    return values.at[tuple(place)].set(largest)


def steps_of(key, extent, shards, low, top_value):
    gain = 1.0
    for position, shards_of in shards:
        steps = jax.random.uniform(jax.random.fold_in(jax.random.fold_in(key, 6), position), (shards_of,), jnp.float32, low / len(shards), top_value / len(shards))
        gain = gain * jnp.repeat(jnp.exp(steps), extent[position] // shards_of).reshape((-1,) + (1,) * (len(extent) - 1 - position))
    return gain


def noise(stream_key, dims, deviation, most, shards=(), kind=jnp.bfloat16):
    values = jax.random.normal(stream_key, dims, jnp.float32) * deviation
    if len(shards) > 0:
        values = steps_of(stream_key, dims, shards, -0.22, 0.18) * values
    return jnp.clip(values, min=-most, max=most).astype(kind)


def setup_inputs(seed: int = 0) -> dict:
    splits = jax.random.split(jax.random.key(seed), 7)
    vertex_times = plant(jax.random.randint(splits[0], (NW, NV), 0, NT), jax.random.fold_in(splits[0], 1), 0, NT - 1).astype(jnp.int32)
    vertex_sites = plant(jax.random.randint(splits[1], (NW, NV), 0, NM), jax.random.fold_in(splits[1], 1), 0, NM - 1).astype(jnp.int32)
    vertex_matrix = noise(splits[2], (NW, NV, NV), NV ** -0.5, 0.1875, ((0, 16), (1, 16)))
    bare_green = noise(splits[3], (2, KS), 0.5, 3.0, (), jnp.float32)
    transfer_momentum = jax.random.permutation(splits[4], NM).astype(jnp.int32)
    transfers = jax.random.permutation(splits[5], NQ).astype(jnp.int32)
    return {"vertex_times": vertex_times, "vertex_sites": vertex_sites, "vertex_matrix": vertex_matrix, "bare_green": bare_green, "transfer_momentum": transfer_momentum, "transfers": transfers}


side_length = 4


def fourier_table(times, sites):
    points = jnp.arange(NM * NF, dtype=jnp.int32)
    momentum = points // NF
    frequency = points % NF
    momentum_x = momentum // side_length
    momentum_y = momentum % side_length
    site_x = sites // side_length
    site_y = sites % side_length
    odd_part = 4 * (2 * frequency + 1 - NF)
    phase = odd_part[:, None] * times[None, :] - 2 * NT * (momentum_x[:, None] * site_x[None, :] + momentum_y[:, None] * site_y[None, :])
    phase = jnp.mod(phase, 8 * NT)
    angle = phase.astype(jnp.float32) * (2.0 * math.pi / (8 * NT))
    return jnp.cos(angle).astype(jnp.bfloat16), jnp.sin(angle).astype(jnp.bfloat16)


def assemble(spread_re, spread_im, row_re, row_im, col_re, col_im, rows, cols):
    scale = NV ** -0.5
    part_re = (spread_re * col_re[None, :] - spread_im * col_im[None, :]) * scale
    part_im = (spread_re * col_im[None, :] + spread_im * col_re[None, :]) * scale
    diagonal = (rows[:, None] == cols[None, :]).astype(jnp.float32)
    green_re = row_re[:, None] * (part_re + diagonal) - row_im[:, None] * part_im
    green_im = row_re[:, None] * part_im + row_im[:, None] * (part_re + diagonal)
    return green_re.astype(jnp.bfloat16), green_im.astype(jnp.bfloat16)


def matmul(left, right):
    return jnp.dot(left, right, preferred_element_type=jnp.float32, precision=lax.Precision.HIGHEST)


def bf16_round(value):
    return lax.optimization_barrier(value.astype(jnp.bfloat16)).astype(jnp.float32)


def walker_green(times, sites, matrix, bare_green):
    four_re, four_im = fourier_table(times, sites)
    fre = four_re.astype(jnp.float32)
    fim = four_im.astype(jnp.float32)
    mat = matrix.astype(jnp.float32)
    inner_re = bf16_round(matmul(fre, mat))
    inner_im = bf16_round(matmul(fim, mat))
    spread_re = matmul(inner_re, fre.T) + matmul(inner_im, fim.T)
    spread_im = matmul(inner_im, fre.T) - matmul(inner_re, fim.T)
    points = jnp.arange(NM * NF, dtype=jnp.int32)
    green_re, green_im = assemble(spread_re, spread_im, bare_green[0], bare_green[1], bare_green[0], bare_green[1], points, points)
    return jnp.stack([green_re, green_im])


def reference(vertex_times, vertex_sites, vertex_matrix, bare_green, transfer_momentum, transfers):
    greens = lax.map(lambda item: walker_green(item[0], item[1], item[2], bare_green), (vertex_times, vertex_sites, vertex_matrix))
    walkers = greens.shape[0]
    shift = transfer_momentum.astype(jnp.int32)
    grid = greens.reshape(walkers, 2, NM, NF, NM, NF)
    moved = jnp.take(jnp.take(grid, shift, axis=2), shift, axis=4)
    turned = jnp.transpose(moved, (0, 1, 4, 5, 2, 3))
    direct = grid.astype(jnp.float32)

    def one_transfer(offset):
        spots = jnp.arange(NF, dtype=jnp.int32) + offset
        valid = ((spots >= 0) & (spots < NF)).astype(jnp.float32)
        clipped = jnp.clip(spots, 0, NF - 1)
        picked = jnp.take(jnp.take(turned, clipped, axis=3), clipped, axis=5).astype(jnp.float32)
        picked = picked * (valid[:, None, None] * valid[None, None, :])
        prod_re = jnp.sum(direct[:, 0] * picked[:, 0] - direct[:, 1] * picked[:, 1], axis=0)
        prod_im = jnp.sum(direct[:, 0] * picked[:, 1] + direct[:, 1] * picked[:, 0], axis=0)
        return jnp.stack([prod_re, prod_im]).reshape(2, NM * NF, NM * NF)

    offsets = transfers - NQ // 2
    result = lax.map(one_transfer, offsets)
    return jnp.transpose(result, (1, 0, 2, 3))
```

```python
import math

import jax
import jax.numpy as jnp
from jax import lax
from jax.experimental import pallas as pl
from jax.experimental.pallas import tpu as pltpu
from jax.sharding import PartitionSpec as P

NM = 16
NF = 64
NV = 1024
NT = 4096
NQ = 32
SIDE = 4
ND = 16
PACK = 2 * NF
TURN = 8 * NT
QUARTER = TURN // 4
MESH = pl.DeviceIdType.MESH
F32 = jnp.float32
BF16 = jnp.bfloat16


def sincos(phase):
    quadrant = (phase + QUARTER // 2) >> 13
    angle = (phase - (quadrant << 13)).astype(F32) * (2.0 * math.pi / TURN)
    square = angle * angle
    sine = angle * (
        1.0 + square * (-1.0 / 6 + square * (1.0 / 120 + square * (-1.0 / 5040 + square * (1.0 / 362880))))
    )
    cosine = 1.0 + square * (
        -0.5 + square * (1.0 / 24 + square * (-1.0 / 720 + square * (1.0 / 40320 - square * (1.0 / 3628800))))
    )
    odd = (quadrant & 1) == 1
    sign = (1 - (quadrant & 2)).astype(F32)
    return jnp.where(odd, -sine, cosine) * sign, jnp.where(odd, cosine, sine) * sign


def swap(value):
    return pltpu.roll(value, NF, 1)


def kernel(
    times,
    sites,
    matrix,
    bare,
    shift,
    transfers,
    out,
    base,
    table,
    outer_re,
    outer_im,
    inverse,
    send_a,
    recv_a,
    green,
    send_t,
    recv_d,
    recv_t,
    direct_re,
    direct_im,
    turned_re,
    turned_im,
    send_o,
    recv_o,
    sem_sa,
    sem_ra,
    sem_sd,
    sem_rd,
    sem_st,
    sem_rt,
    sem_so,
    sem_ro,
):
    w = lax.axis_index("walk")
    b = lax.axis_index("blk")
    source = lax.rem(b - w + ND, ND)
    twice = lax.rem(2 * w, ND)
    alone = twice == b

    barrier = pltpu.get_barrier_semaphore()

    def greet(i, carry):
        pl.semaphore_signal(barrier, inc=1, device_id=(lax.rem(w + i, ND), b), device_id_type=MESH)
        pl.semaphore_signal(barrier, inc=1, device_id=(w, lax.rem(b + i, ND)), device_id_type=MESH)
        return carry

    lax.fori_loop(1, ND, greet, 0)

    def greet_source(i, carry):
        @pl.when(jnp.logical_not(jnp.logical_and(alone, i == b)))
        def _():
            pl.semaphore_signal(barrier, inc=1, device_id=(source, i), device_id_type=MESH)

        return carry

    lax.fori_loop(0, ND, greet_source, 0)

    def base_rows(i, carry):
        first = pl.multiple_of(i * 16, 16)
        f = lax.broadcasted_iota(jnp.int32, (16, NV), 0) + first
        phase = (4 * (2 * f + 1 - NF) * times[...]) & (TURN - 1)
        cosine, sine = sincos(phase)
        base[0, pl.ds(first, 16), :] = cosine.astype(BF16)
        base[1, pl.ds(first, 16), :] = sine.astype(BF16)
        return carry

    lax.fori_loop(0, NF // 16, base_rows, 0)

    def rotate(m, carry):
        turn = ((m // SIDE) * (sites[...] >> 2) + (m % SIDE) * (sites[...] & 3)) & 3
        sign = (1 - (turn & 2)).astype(F32)
        odd = (turn & 1).astype(F32)
        along = jnp.broadcast_to((1.0 - odd) * sign, (NF, NV)).astype(BF16)
        across = jnp.broadcast_to(odd * sign, (NF, NV)).astype(BF16)
        cosine = base[0]
        sine = base[1]
        table[m, 0:NF, :] = cosine * along + sine * across
        table[m, NF:PACK, :] = sine * along - cosine * across
        return carry

    lax.fori_loop(0, NM, rotate, 0)

    def project(i, carry):
        block = lax.dot_general(
            matrix[0], table[shift[i]], (((1,), (1,)), ((), ())), preferred_element_type=F32
        )
        send_a[i] = block.astype(BF16)
        return carry

    lax.fori_loop(0, ND, project, 0)

    pl.semaphore_wait(barrier, 3 * ND - 2 - alone.astype(jnp.int32))

    def copy_a(peer):
        return pltpu.make_async_remote_copy(
            src_ref=send_a.at[peer],
            dst_ref=recv_a.at[pl.ds(pl.multiple_of(w * NF, NF), NF)],
            send_sem=sem_sa.at[peer],
            recv_sem=sem_ra.at[w],
            device_id=(peer, b),
            device_id_type=MESH,
        )

    def start_a(i, carry):
        copy_a(lax.rem(w + i, ND)).start()
        return carry

    lax.fori_loop(1, ND, start_a, 0)
    recv_a[pl.ds(pl.multiple_of(w * NF, NF), NF), :] = send_a[w]

    for part, target in ((0, outer_re), (1, outer_im)):
        for tile in range(NV // 128):
            row = jnp.broadcast_to(bare[part : part + 1, tile * 128 : tile * 128 + 128], (128, 128))
            target[tile * 128 : tile * 128 + 128, :] = row.T

    for m in range(NM):
        position = jnp.int32(0)
        for i in range(1, NM):
            position = jnp.where(shift[i] == m, i, position)
        inverse[m] = position

    for target in (turned_re, turned_im):
        for pair in range(NM // 2):
            target[pair, 0:16, :] = jnp.zeros((16, 128), F32)
            target[pair, 80:96, :] = jnp.zeros((16, 128), F32)

    left = lax.broadcasted_iota(jnp.int32, (NF, PACK), 1) < NF
    row_of = lax.broadcasted_iota(jnp.int32, (NF, PACK), 0)
    lane_of = lax.broadcasted_iota(jnp.int32, (NF, PACK), 1) & (NF - 1)
    minus_right = jnp.where(left, 1.0, -1.0)
    minus_left = -minus_right
    mine = shift[w]
    col_re = bare[0:1, 0:NF]
    col_im = bare[1:2, 0:NF]
    for m in range(1, NM):
        col_re = jnp.where(mine == m, bare[0:1, m * NF : m * NF + NF], col_re)
        col_im = jnp.where(mine == m, bare[1:2, m * NF : m * NF + NF], col_im)
    scale = NV ** (-0.5)
    col_re = jnp.concatenate([col_re, col_re], axis=1) * scale
    col_im = jnp.concatenate([-col_im, col_im], axis=1) * scale

    def arrive_a(i, carry):
        peer = lax.rem(w + i, ND)
        pltpu.make_async_remote_copy(
            src_ref=send_a.at[peer],
            dst_ref=recv_a.at[pl.ds(pl.multiple_of(peer * NF, NF), NF)],
            send_sem=sem_sa.at[peer],
            recv_sem=sem_ra.at[peer],
            device_id=(peer, b),
            device_id_type=MESH,
        ).wait()
        return carry

    lax.fori_loop(1, ND, arrive_a, 0)

    def copy_d(m):
        return pltpu.make_async_remote_copy(
            src_ref=green.at[m],
            dst_ref=recv_d.at[b],
            send_sem=sem_sd.at[m],
            recv_sem=sem_rd.at[b],
            device_id=(m, lax.rem(w + m, ND)),
            device_id_type=MESH,
        )

    def own_d(m):
        return pltpu.make_async_copy(green.at[m], recv_d.at[b], sem_rd.at[b])

    def is_own(m):
        return jnp.logical_and(alone, m == w)

    def assemble(group, carry):
        first = group * 4
        rows = table[pl.ds(first, 4)].reshape(4 * PACK, NV)
        raw = jnp.dot(rows, recv_a[...], preferred_element_type=F32)
        for k in range(4):
            m = first + k
            spread = raw[k * PACK : k * PACK + NF] * minus_right + swap(raw[k * PACK + NF : (k + 1) * PACK])
            part = spread * col_re + swap(spread) * col_im
            part = part + jnp.where(jnp.logical_and(left, row_of == lane_of), (mine == m).astype(F32), 0.0)
            start = pl.multiple_of(m * NF, NF)
            value = outer_re[pl.ds(start, NF), :] * part + outer_im[pl.ds(start, NF), :] * minus_left * swap(part)
            green[m] = value.astype(BF16)
        for k in range(4):
            m = first + k

            @pl.when(jnp.logical_not(is_own(m)))
            def _():
                copy_d(m).start()

            @pl.when(is_own(m))
            def _():
                own_d(m).start()

        return carry

    lax.fori_loop(0, NM // 4, assemble, 0)

    def copy_t(peer):
        return pltpu.make_async_remote_copy(
            src_ref=send_t.at[peer],
            dst_ref=recv_t.at[b],
            send_sem=sem_st.at[peer],
            recv_sem=sem_rt.at[b],
            device_id=(w, peer),
            device_id_type=MESH,
        )

    def start_t(i, carry):
        peer = lax.rem(b + i, ND)
        send_t[peer] = green[shift[shift[lax.rem(peer - w + ND, ND)]]]
        copy_t(peer).start()
        return carry

    lax.fori_loop(1, ND, start_t, 0)
    recv_t[b] = green[shift[shift[source]]]

    def arrive_b(u, carry):
        pltpu.make_async_copy(green.at[0], recv_d.at[u], sem_rd.at[u]).wait()

        @pl.when(u != b)
        def _():
            pltpu.make_async_copy(green.at[0], recv_t.at[u], sem_rt.at[u]).wait()

        return carry

    def pair_up(pair, carry):
        arrive_b(2 * pair, 0)
        arrive_b(2 * pair + 1, 0)
        even = recv_d[2 * pair].astype(F32)
        other = recv_d[2 * pair + 1].astype(F32)
        direct_re[pair] = jnp.where(left, even, swap(other))
        direct_im[pair] = jnp.where(left, swap(even), other)
        both = recv_t[pl.ds(2 * pair, 2)].astype(F32).reshape(2 * NF, PACK).T
        turned_re[pair, 16 : 16 + NF, :] = both[0:NF]
        turned_im[pair, 16 : 16 + NF, :] = both[NF:PACK]
        return carry

    lax.fori_loop(0, NM // 2, pair_up, 0)

    def copy_o(peer):
        return pltpu.make_async_remote_copy(
            src_ref=send_o.at[peer],
            dst_ref=recv_o.at[b],
            send_sem=sem_so.at[peer],
            recv_sem=sem_ro.at[b],
            device_id=(w, peer),
            device_id_type=MESH,
        )

    def window(i, carry):
        peer = lax.rem(b + i, ND)
        for k in range(2):
            offset = transfers[2 * peer + k]
            turn = (PACK + NQ // 2 - offset) & (PACK - 1)
            sum_re = jnp.zeros((NF, PACK), F32)
            sum_im = jnp.zeros((NF, PACK), F32)
            for pair in range(NM // 2):
                near_re = direct_re[pair]
                near_im = direct_im[pair]
                far_re = pltpu.roll(turned_re[pair, pl.ds(offset, NF), :], turn, 1)
                far_im = pltpu.roll(turned_im[pair, pl.ds(offset, NF), :], turn, 1)
                sum_re = sum_re + (near_re * far_re - near_im * far_im)
                sum_im = sum_im + (near_re * far_im + near_im * far_re)
            sum_re = sum_re + swap(sum_re)
            sum_im = sum_im + swap(sum_im)
            nu = offset - NQ // 2
            row = row_of + nu
            col = lane_of + nu
            keep = (row >= 0) & (row < NF) & (col >= 0) & (col < NF)
            send_o[peer, k] = jnp.where(keep, jnp.where(left, sum_re, sum_im), 0.0).astype(BF16)

        @pl.when(i < ND)
        def _():
            copy_o(peer).start()

        return carry

    lax.fori_loop(1, ND + 1, window, 0)
    recv_o[b] = send_o[b]

    def arrive_o(i, carry):
        peer = lax.rem(b + i, ND)
        pltpu.make_async_copy(send_o.at[peer], recv_o.at[peer], sem_ro.at[peer]).wait()
        return carry

    lax.fori_loop(1, ND, arrive_o, 0)

    for tile in range(NM // 2):
        even = recv_o[lax.rem(inverse[2 * tile] + w, ND)].astype(F32)
        other = recv_o[lax.rem(inverse[2 * tile + 1] + w, ND)].astype(F32)
        for k in range(2):
            out[0, k, :, tile * 128 : tile * 128 + 128] = jnp.where(left, even[k], swap(other[k]))
            out[1, k, :, tile * 128 : tile * 128 + 128] = jnp.where(left, swap(even[k]), other[k])

    def drain(i, carry):
        peer = lax.rem(b + i, ND)
        copy_t(peer).wait_send()
        copy_o(peer).wait_send()
        return carry

    lax.fori_loop(1, ND, drain, 0)

    def drain_d(m, carry):
        @pl.when(jnp.logical_not(is_own(m)))
        def _():
            copy_d(m).wait_send()

        return carry

    lax.fori_loop(0, NM, drain_d, 0)


def shards(vertex_times, vertex_sites, vertex_matrix, bare_green, transfer_momentum, transfers):
    vmem = pl.BlockSpec(memory_space=pltpu.VMEM)
    smem = pl.BlockSpec(memory_space=pltpu.SMEM)
    sems = pltpu.SemaphoreType.DMA((ND,))
    blocks = pltpu.VMEM((ND, NF, PACK), BF16)
    return pl.pallas_call(
        kernel,
        out_shape=jax.ShapeDtypeStruct((2, 2, NF, NV), F32),
        in_specs=[vmem, vmem, vmem, vmem, smem, smem],
        out_specs=vmem,
        scratch_shapes=[
            pltpu.VMEM((2, NF, NV), BF16),
            pltpu.VMEM((NM, PACK, NV), BF16),
            pltpu.VMEM((NV, PACK), F32),
            pltpu.VMEM((NV, PACK), F32),
            pltpu.SMEM((NM,), jnp.int32),
            blocks,
            pltpu.VMEM((NV, PACK), BF16),
            blocks,
            blocks,
            blocks,
            blocks,
            pltpu.VMEM((NM // 2, NF, PACK), F32),
            pltpu.VMEM((NM // 2, NF, PACK), F32),
            pltpu.VMEM((NM // 2, NF + 32, PACK), F32),
            pltpu.VMEM((NM // 2, NF + 32, PACK), F32),
            pltpu.VMEM((ND, 2, NF, PACK), BF16),
            pltpu.VMEM((ND, 2, NF, PACK), BF16),
        ]
        + [sems] * 8,
        compiler_params=pltpu.CompilerParams(collective_id=0, has_side_effects=True),
    )(vertex_times, vertex_sites, vertex_matrix, bare_green, transfer_momentum, transfers)


def solution(mesh):
    return jax.shard_map(
        shards,
        mesh=mesh,
        in_specs=(P("blk", None), P("blk", None), P("blk", "walk", None), P(), P(), P()),
        out_specs=P(None, "blk", "walk", None),
        check_vma=False,
    )
```

```python
import math

import jax
import jax.numpy as jnp
from jax import lax
from jax.experimental import pallas as pl
from jax.experimental.pallas import tpu as pltpu
from jax.sharding import PartitionSpec as P

NM = 16
NF = 64
NV = 1024
NT = 4096
NQ = 32
SIDE = 4
ND = 16
PACK = 2 * NF
TURN = 8 * NT
QUARTER = TURN // 4
MESH = pl.DeviceIdType.MESH
F32 = jnp.float32
BF16 = jnp.bfloat16


def sincos(phase):
    quadrant = (phase + QUARTER // 2) >> 13
    angle = (phase - (quadrant << 13)).astype(F32) * (2.0 * math.pi / TURN)
    square = angle * angle
    sine = angle * (
        1.0 + square * (-1.0 / 6 + square * (1.0 / 120 + square * (-1.0 / 5040 + square * (1.0 / 362880))))
    )
    cosine = 1.0 + square * (
        -0.5 + square * (1.0 / 24 + square * (-1.0 / 720 + square * (1.0 / 40320 - square * (1.0 / 3628800))))
    )
    odd = (quadrant & 1) == 1
    sign = (1 - (quadrant & 2)).astype(F32)
    return jnp.where(odd, -sine, cosine) * sign, jnp.where(odd, cosine, sine) * sign


def swap(value):
    return pltpu.roll(value, NF, 1)


def kernel(
    times,
    sites,
    matrix,
    bare,
    shift,
    transfers,
    out,
    base,
    table,
    outer_re,
    outer_im,
    inverse,
    send_a,
    recv_a,
    green,
    send_t,
    recv_d,
    recv_t,
    direct_re,
    direct_im,
    turned_re,
    turned_im,
    send_o,
    recv_o,
    sem_sa,
    sem_ra,
    sem_sd,
    sem_rd,
    sem_st,
    sem_rt,
    sem_so,
    sem_ro,
):
    w = lax.axis_index("walk")
    b = lax.axis_index("blk")
    source = lax.rem(b - w + ND, ND)
    alone = source == w

    def along_walk(i):
        step = i // 2
        far = (step + 1) // 2
        z = w // 2 + 4 + far - 2 * far * (step % 2)
        return lax.rem(z + 8, 8) * 2 + lax.rem(w + i + 1, 2)

    def along_blk(i):
        step = i // 4
        y = (b // 2) % 4 + jnp.where(step == 0, 2, jnp.where(step == 1, 1, jnp.where(step == 2, 3, 0)))
        x = b // 8 + 1 - (i % 4) // 2
        return lax.rem(x, 2) * 8 + lax.rem(y, 4) * 2 + lax.rem(b + i + 1, 2)

    barrier = pltpu.get_barrier_semaphore()

    def greet(i, carry):
        pl.semaphore_signal(barrier, inc=1, device_id=(lax.rem(w + i, ND), b), device_id_type=MESH)
        pl.semaphore_signal(barrier, inc=1, device_id=(w, lax.rem(b + i, ND)), device_id_type=MESH)
        return carry

    lax.fori_loop(1, ND, greet, 0)

    def base_rows(i, carry):
        first = pl.multiple_of(i * 16, 16)
        f = lax.broadcasted_iota(jnp.int32, (16, NV), 0) + first
        phase = (4 * (2 * f + 1 - NF) * times[...]) & (TURN - 1)
        cosine, sine = sincos(phase)
        base[0, pl.ds(first, 16), :] = cosine.astype(BF16)
        base[1, pl.ds(first, 16), :] = sine.astype(BF16)
        return carry

    lax.fori_loop(0, NF // 16, base_rows, 0)

    def rotate(m, carry):
        turn = ((m // SIDE) * (sites[...] >> 2) + (m % SIDE) * (sites[...] & 3)) & 3
        sign = (1 - (turn & 2)).astype(F32)
        odd = (turn & 1).astype(F32)
        along = jnp.broadcast_to((1.0 - odd) * sign, (NF, NV)).astype(BF16)
        across = jnp.broadcast_to(odd * sign, (NF, NV)).astype(BF16)
        cosine = base[0]
        sine = base[1]
        table[m, 0:NF, :] = cosine * along + sine * across
        table[m, NF:PACK, :] = sine * along - cosine * across
        return carry

    lax.fori_loop(0, NM, rotate, 0)

    def project(i, carry):
        block = lax.dot_general(
            matrix[0], table[shift[i]], (((1,), (1,)), ((), ())), preferred_element_type=F32
        )
        send_a[i] = block.astype(BF16)
        return carry

    lax.fori_loop(0, ND, project, 0)

    pl.semaphore_wait(barrier, 2 * ND - 2)

    def copy_a(peer):
        return pltpu.make_async_remote_copy(
            src_ref=send_a.at[peer],
            dst_ref=recv_a.at[pl.ds(pl.multiple_of(w * NF, NF), NF)],
            send_sem=sem_sa.at[peer],
            recv_sem=sem_ra.at[w],
            device_id=(peer, b),
            device_id_type=MESH,
        )

    def start_a(i, carry):
        copy_a(along_walk(i)).start()
        return carry

    lax.fori_loop(0, ND - 1, start_a, 0)
    recv_a[pl.ds(pl.multiple_of(w * NF, NF), NF), :] = send_a[w]

    for part, target in ((0, outer_re), (1, outer_im)):
        for tile in range(NV // 128):
            row = jnp.broadcast_to(bare[part : part + 1, tile * 128 : tile * 128 + 128], (128, 128))
            target[tile * 128 : tile * 128 + 128, :] = row.T

    for m in range(NM):
        position = jnp.int32(0)
        for i in range(1, NM):
            position = jnp.where(shift[i] == m, i, position)
        inverse[m] = position

    for target in (turned_re, turned_im):
        for pair in range(NM // 2):
            target[pair, 0:16, :] = jnp.zeros((16, 128), F32)
            target[pair, 80:96, :] = jnp.zeros((16, 128), F32)

    left = lax.broadcasted_iota(jnp.int32, (NF, PACK), 1) < NF
    row_of = lax.broadcasted_iota(jnp.int32, (NF, PACK), 0)
    lane_of = lax.broadcasted_iota(jnp.int32, (NF, PACK), 1) & (NF - 1)
    minus_right = jnp.where(left, 1.0, -1.0)
    minus_left = -minus_right
    mine = shift[w]
    col_re = bare[0:1, 0:NF]
    col_im = bare[1:2, 0:NF]
    for m in range(1, NM):
        col_re = jnp.where(mine == m, bare[0:1, m * NF : m * NF + NF], col_re)
        col_im = jnp.where(mine == m, bare[1:2, m * NF : m * NF + NF], col_im)
    scale = NV ** (-0.5)
    col_re = jnp.concatenate([col_re, col_re], axis=1) * scale
    col_im = jnp.concatenate([-col_im, col_im], axis=1) * scale

    def arrive_a(i, carry):
        peer = lax.rem(w + i, ND)
        pltpu.make_async_remote_copy(
            src_ref=send_a.at[peer],
            dst_ref=recv_a.at[pl.ds(pl.multiple_of(peer * NF, NF), NF)],
            send_sem=sem_sa.at[peer],
            recv_sem=sem_ra.at[peer],
            device_id=(peer, b),
            device_id_type=MESH,
        ).wait()
        return carry

    lax.fori_loop(1, ND, arrive_a, 0)

    def copy_d(m):
        return pltpu.make_async_remote_copy(
            src_ref=green.at[m],
            dst_ref=recv_d.at[b],
            send_sem=sem_sd.at[m],
            recv_sem=sem_rd.at[b],
            device_id=(m, lax.rem(w + m, ND)),
            device_id_type=MESH,
        )

    def own_d(m):
        return pltpu.make_async_copy(green.at[m], recv_d.at[b], sem_rd.at[b])

    def is_own(m):
        return jnp.logical_and(alone, m == w)

    def assemble(group, carry):
        momenta = [4 * group + k for k in range(4)]
        rows = jnp.concatenate([table[m] for m in momenta], axis=0)
        raw = jnp.dot(rows, recv_a[...], preferred_element_type=F32)
        for k, m in enumerate(momenta):
            spread = raw[k * PACK : k * PACK + NF] * minus_right + swap(raw[k * PACK + NF : (k + 1) * PACK])
            part = spread * col_re + swap(spread) * col_im
            part = part + jnp.where(jnp.logical_and(left, row_of == lane_of), (mine == m).astype(F32), 0.0)
            start = pl.multiple_of(m * NF, NF)
            value = outer_re[pl.ds(start, NF), :] * part + outer_im[pl.ds(start, NF), :] * minus_left * swap(part)
            green[m] = value.astype(BF16)
        for m in momenta:

            @pl.when(jnp.logical_not(is_own(m)))
            def _():
                copy_d(m).start()

            @pl.when(is_own(m))
            def _():
                own_d(m).start()

        return carry

    lax.fori_loop(0, NM // 4, assemble, 0)

    def copy_t(peer):
        return pltpu.make_async_remote_copy(
            src_ref=send_t.at[peer],
            dst_ref=recv_t.at[b],
            send_sem=sem_st.at[peer],
            recv_sem=sem_rt.at[b],
            device_id=(w, peer),
            device_id_type=MESH,
        )

    def start_t(i, carry):
        peer = along_blk(i)
        send_t[peer] = green[shift[shift[lax.rem(peer - w + ND, ND)]]]
        copy_t(peer).start()
        return carry

    lax.fori_loop(0, ND - 1, start_t, 0)
    recv_t[b] = green[shift[shift[source]]]

    def arrive_b(u, carry):
        pltpu.make_async_copy(green.at[0], recv_d.at[u], sem_rd.at[u]).wait()

        @pl.when(u != b)
        def _():
            pltpu.make_async_copy(green.at[0], recv_t.at[u], sem_rt.at[u]).wait()

        return carry

    def pair_up(pair, carry):
        arrive_b(2 * pair, 0)
        arrive_b(2 * pair + 1, 0)
        even = recv_d[2 * pair].astype(F32)
        other = recv_d[2 * pair + 1].astype(F32)
        direct_re[pair] = jnp.where(left, even, swap(other))
        direct_im[pair] = jnp.where(left, swap(even), other)
        both = recv_t[pl.ds(2 * pair, 2)].astype(F32).reshape(2 * NF, PACK).T
        turned_re[pair, 16 : 16 + NF, :] = both[0:NF]
        turned_im[pair, 16 : 16 + NF, :] = both[NF:PACK]
        return carry

    lax.fori_loop(0, NM // 2, pair_up, 0)

    def copy_o(peer):
        return pltpu.make_async_remote_copy(
            src_ref=send_o.at[peer],
            dst_ref=recv_o.at[b],
            send_sem=sem_so.at[peer],
            recv_sem=sem_ro.at[b],
            device_id=(w, peer),
            device_id_type=MESH,
        )

    def window(i, carry):
        peer = along_blk(i)
        for k in range(2):
            offset = transfers[2 * peer + k]
            turn = (PACK + NQ // 2 - offset) & (PACK - 1)
            sum_re = jnp.zeros((NF, PACK), F32)
            sum_im = jnp.zeros((NF, PACK), F32)
            for pair in range(NM // 2):
                near_re = direct_re[pair]
                near_im = direct_im[pair]
                far_re = pltpu.roll(turned_re[pair, pl.ds(offset, NF), :], turn, 1)
                far_im = pltpu.roll(turned_im[pair, pl.ds(offset, NF), :], turn, 1)
                sum_re = sum_re + (near_re * far_re - near_im * far_im)
                sum_im = sum_im + (near_re * far_im + near_im * far_re)
            sum_re = sum_re + swap(sum_re)
            sum_im = sum_im + swap(sum_im)
            nu = offset - NQ // 2
            row = row_of + nu
            col = lane_of + nu
            keep = (row >= 0) & (row < NF) & (col >= 0) & (col < NF)
            send_o[peer, k] = jnp.where(keep, jnp.where(left, sum_re, sum_im), 0.0).astype(BF16)

        @pl.when(i < ND - 1)
        def _():
            copy_o(peer).start()

        return carry

    lax.fori_loop(0, ND, window, 0)
    recv_o[b] = send_o[b]

    def arrive_o(i, carry):
        peer = lax.rem(b + i, ND)
        pltpu.make_async_copy(send_o.at[peer], recv_o.at[peer], sem_ro.at[peer]).wait()
        return carry

    lax.fori_loop(1, ND, arrive_o, 0)

    for tile in range(NM // 2):
        even = recv_o[lax.rem(inverse[2 * tile] + w, ND)].astype(F32)
        other = recv_o[lax.rem(inverse[2 * tile + 1] + w, ND)].astype(F32)
        for k in range(2):
            out[0, k, :, tile * 128 : tile * 128 + 128] = jnp.where(left, even[k], swap(other[k]))
            out[1, k, :, tile * 128 : tile * 128 + 128] = jnp.where(left, swap(even[k]), other[k])

    def drain(i, carry):
        peer = lax.rem(b + i, ND)
        copy_t(peer).wait_send()
        copy_o(peer).wait_send()
        return carry

    lax.fori_loop(1, ND, drain, 0)

    def drain_d(m, carry):
        @pl.when(jnp.logical_not(is_own(m)))
        def _():
            copy_d(m).wait_send()

        return carry

    lax.fori_loop(0, NM, drain_d, 0)


def shards(vertex_times, vertex_sites, vertex_matrix, bare_green, transfer_momentum, transfers):
    vmem = pl.BlockSpec(memory_space=pltpu.VMEM)
    smem = pl.BlockSpec(memory_space=pltpu.SMEM)
    sems = pltpu.SemaphoreType.DMA((ND,))
    blocks = pltpu.VMEM((ND, NF, PACK), BF16)
    return pl.pallas_call(
        kernel,
        out_shape=jax.ShapeDtypeStruct((2, 2, NF, NV), F32),
        in_specs=[vmem, vmem, vmem, vmem, smem, smem],
        out_specs=vmem,
        scratch_shapes=[
            pltpu.VMEM((2, NF, NV), BF16),
            pltpu.VMEM((NM, PACK, NV), BF16),
            pltpu.VMEM((NV, PACK), F32),
            pltpu.VMEM((NV, PACK), F32),
            pltpu.SMEM((NM,), jnp.int32),
            blocks,
            pltpu.VMEM((NV, PACK), BF16),
            blocks,
            blocks,
            blocks,
            blocks,
            pltpu.VMEM((NM // 2, NF, PACK), F32),
            pltpu.VMEM((NM // 2, NF, PACK), F32),
            pltpu.VMEM((NM // 2, NF + 32, PACK), F32),
            pltpu.VMEM((NM // 2, NF + 32, PACK), F32),
            pltpu.VMEM((ND, 2, NF, PACK), BF16),
            pltpu.VMEM((ND, 2, NF, PACK), BF16),
        ]
        + [sems] * 8,
        compiler_params=pltpu.CompilerParams(collective_id=0, has_side_effects=True),
    )(vertex_times, vertex_sites, vertex_matrix, bare_green, transfer_momentum, transfers)


def solution(mesh):
    return jax.shard_map(
        shards,
        mesh=mesh,
        in_specs=(P("blk", None), P("blk", None), P("blk", "walk", None), P(), P(), P()),
        out_specs=P(None, "blk", "walk", None),
        check_vma=False,
    )
```

```python
import math

import jax
import jax.numpy as jnp
from jax import lax
from jax.experimental import pallas as pl
from jax.experimental.pallas import tpu as pltpu
from jax.sharding import PartitionSpec as P

NM = 16
NF = 64
NV = 1024
NT = 4096
NQ = 32
SIDE = 4
ND = 16
PACK = 2 * NF
TURN = 8 * NT
QUARTER = TURN // 4
BAND = 16
MESH = pl.DeviceIdType.MESH
F32 = jnp.float32
BF16 = jnp.bfloat16


def sincos(phase):
    quadrant = (phase + QUARTER // 2) >> 13
    angle = (phase - (quadrant << 13)).astype(F32) * (2.0 * math.pi / TURN)
    square = angle * angle
    sine = angle * (
        1.0 + square * (-1.0 / 6 + square * (1.0 / 120 + square * (-1.0 / 5040 + square * (1.0 / 362880))))
    )
    cosine = 1.0 + square * (
        -0.5 + square * (1.0 / 24 + square * (-1.0 / 720 + square * (1.0 / 40320 - square * (1.0 / 3628800))))
    )
    odd = (quadrant & 1) == 1
    sign = (1 - (quadrant & 2)).astype(F32)
    return jnp.where(odd, -sine, cosine) * sign, jnp.where(odd, cosine, sine) * sign


def pick(value, lanes):
    return jnp.take_along_axis(value, lanes, axis=1)


def swap(value):
    return pltpu.roll(value, NF, 1)


def kernel(
    times_in,
    sites_in,
    matrix_in,
    bare_in,
    shift_in,
    transfers_in,
    out,
    inverse,
    times,
    sites,
    matrix,
    bare,
    shift,
    transfers,
    base,
    table,
    outer_re,
    outer_im,
    tables,
    chosen,
    send_a,
    recv_a,
    green,
    send_d,
    send_t,
    recv_d,
    recv_t,
    direct_re,
    direct_im,
    turned_re,
    turned_im,
    total,
    send_o,
    sem_in,
    sem_sa,
    sem_ra,
    sem_sd,
    sem_rd,
    sem_st,
    sem_rt,
    sem_so,
    sem_ro,
):
    w = lax.axis_index("walk")
    b = lax.axis_index("blk")
    source = lax.rem(b - w + ND, ND)
    alone = source == w

    def along_walk(i):
        step = i // 2
        far = (step + 1) // 2
        z = w // 2 + 4 + far - 2 * far * (step % 2)
        return lax.rem(z + 8, 8) * 2 + lax.rem(w + i + 1, 2)

    def along_blk(i):
        step = i // 4
        y = (b // 2) % 4 + jnp.where(step == 0, 2, jnp.where(step == 1, 1, jnp.where(step == 2, 3, 0)))
        x = b // 8 + 1 - (i % 4) // 2
        return lax.rem(x, 2) * 8 + lax.rem(y, 4) * 2 + lax.rem(b + i + 1, 2)

    barrier = pltpu.get_barrier_semaphore()

    def greet(i, carry):
        pl.semaphore_signal(barrier, inc=1, device_id=(lax.rem(w + i, ND), b), device_id_type=MESH)
        pl.semaphore_signal(barrier, inc=1, device_id=(w, lax.rem(b + i, ND)), device_id_type=MESH)
        return carry

    lax.fori_loop(1, ND, greet, 0)

    incoming = [
        pltpu.make_async_copy(held, here, sem_in.at[k])
        for k, (held, here) in enumerate(
            (
                (times_in, times),
                (sites_in, sites),
                (matrix_in, matrix),
                (bare_in, bare),
                (shift_in, shift),
                (transfers_in, transfers),
            )
        )
    ]
    for copy in incoming:
        copy.start()
    for copy in incoming:
        copy.wait()

    def base_rows(i, carry):
        first = pl.multiple_of(i * 16, 16)
        f = lax.broadcasted_iota(jnp.int32, (16, NV), 0) + first
        phase = (4 * (2 * f + 1 - NF) * times[...]) & (TURN - 1)
        cosine, sine = sincos(phase)
        base[0, pl.ds(first, 16), :] = cosine.astype(BF16)
        base[1, pl.ds(first, 16), :] = sine.astype(BF16)
        return carry

    lax.fori_loop(0, NF // 16, base_rows, 0)

    def rotate(m, carry):
        turn = ((m // SIDE) * (sites[...] >> 2) + (m % SIDE) * (sites[...] & 3)) & 3
        sign = (1 - (turn & 2)).astype(F32)
        odd = (turn & 1).astype(F32)
        along = jnp.broadcast_to((1.0 - odd) * sign, (NF, NV)).astype(BF16)
        across = jnp.broadcast_to(odd * sign, (NF, NV)).astype(BF16)
        cosine = base[0]
        sine = base[1]
        table[m, 0:NF, :] = cosine * along + sine * across
        table[m, NF:PACK, :] = sine * along - cosine * across
        return carry

    lax.fori_loop(0, NM, rotate, 0)

    left = lax.broadcasted_iota(jnp.int32, (NF, PACK), 1) < NF
    row_of = lax.broadcasted_iota(jnp.int32, (NF, PACK), 0)
    whole_lane = lax.broadcasted_iota(jnp.int32, (NF, PACK), 1)
    lane_of = whole_lane & (NF - 1)
    skew = (whole_lane & NF) | ((whole_lane + row_of) & (NF - 1))
    straight = (whole_lane & NF) | ((whole_lane - row_of) & (NF - 1))
    minus_left = jnp.where(left, -1.0, 1.0)
    scale = NV ** (-0.5)

    for m in range(NM):
        for part in range(2):
            piece = bare[part : part + 1, m * NF : m * NF + NF]
            tables[m, part : part + 1, :] = jnp.concatenate([piece, -piece if part == 0 else piece], axis=1) * scale

    def project(i, carry):
        m = shift[i]
        block = lax.dot_general(matrix[0], table[m], (((1,), (1,)), ((), ())), preferred_element_type=F32)
        factors = tables[m]
        send_a[i] = (block * factors[0:1] + swap(block) * factors[1:2]).astype(BF16)
        return carry

    lax.fori_loop(0, ND, project, 0)

    pl.semaphore_wait(barrier, 2 * ND - 2)

    def copy_a(peer):
        return pltpu.make_async_remote_copy(
            src_ref=send_a.at[peer],
            dst_ref=recv_a.at[pl.ds(pl.multiple_of(w * NF, NF), NF)],
            send_sem=sem_sa.at[peer],
            recv_sem=sem_ra.at[w],
            device_id=(peer, b),
            device_id_type=MESH,
        )

    def start_a(i, carry):
        copy_a(along_walk(i)).start()
        return carry

    lax.fori_loop(0, ND - 1, start_a, 0)
    recv_a[pl.ds(pl.multiple_of(w * NF, NF), NF), :] = send_a[w]

    for part, target in ((0, outer_re), (1, outer_im)):
        for tile in range(NV // 128):
            row = jnp.broadcast_to(bare[part : part + 1, tile * 128 : tile * 128 + 128], (128, 128))
            column = row.T
            if part == 1:
                column = jnp.where(lax.broadcasted_iota(jnp.int32, (128, 128), 1) < NF, -column, column)
            target[tile * 128 : tile * 128 + 128, :] = column

    for m in range(NM):
        position = jnp.int32(0)
        for i in range(1, NM):
            position = jnp.where(shift[i] == m, i, position)
        inverse[m] = position

    for target in (turned_re, turned_im):
        for pair in range(NM // 2):
            target[pair, 0:16, :] = jnp.zeros((16, 128), F32)
            target[pair, 80:96, :] = jnp.zeros((16, 128), F32)

    mine = shift[w]
    for i in range(ND):
        chosen[i] = shift[shift[lax.rem(along_blk(i) - w + ND, ND)]]

    def arrive_a(i, carry):
        peer = lax.rem(w + i, ND)
        pltpu.make_async_remote_copy(
            src_ref=send_a.at[peer],
            dst_ref=recv_a.at[pl.ds(pl.multiple_of(peer * NF, NF), NF)],
            send_sem=sem_sa.at[peer],
            recv_sem=sem_ra.at[peer],
            device_id=(peer, b),
            device_id_type=MESH,
        ).wait()
        return carry

    lax.fori_loop(1, ND, arrive_a, 0)

    def copy_d(m):
        return pltpu.make_async_remote_copy(
            src_ref=send_d.at[m],
            dst_ref=recv_d.at[b],
            send_sem=sem_sd.at[m],
            recv_sem=sem_rd.at[b],
            device_id=(m, lax.rem(w + m, ND)),
            device_id_type=MESH,
        )

    def own_d(m):
        return pltpu.make_async_copy(send_d.at[m], recv_d.at[b], sem_rd.at[b])

    def is_own(m):
        return jnp.logical_and(alone, m == w)

    diagonal = jnp.where(jnp.logical_and(left, row_of == lane_of), 1.0, 0.0)

    def assemble(group, carry):
        momenta = [4 * group + k for k in range(4)]
        rows = jnp.concatenate([table[m] for m in momenta], axis=0)
        raw = jnp.dot(rows, recv_a[...], preferred_element_type=F32)
        for k, m in enumerate(momenta):
            part = raw[k * PACK : k * PACK + NF] + swap(raw[k * PACK + NF : (k + 1) * PACK]) * minus_left
            part = part + diagonal * (mine == m).astype(F32)
            start = pl.multiple_of(m * NF, NF)
            value = outer_re[pl.ds(start, NF), :] * part + outer_im[pl.ds(start, NF), :] * swap(part)
            green[m] = value.astype(BF16)
            send_d[m] = pick(value, skew).astype(BF16)
        for m in momenta:

            @pl.when(jnp.logical_not(is_own(m)))
            def _():
                copy_d(m).start()

            @pl.when(is_own(m))
            def _():
                own_d(m).start()

        return carry

    lax.fori_loop(0, NM // 4, assemble, 0)

    def copy_t(peer):
        return pltpu.make_async_remote_copy(
            src_ref=send_t.at[peer],
            dst_ref=recv_t.at[b],
            send_sem=sem_st.at[peer],
            recv_sem=sem_rt.at[b],
            device_id=(w, peer),
            device_id_type=MESH,
        )

    def start_t(i, carry):
        peer = along_blk(i)
        send_t[peer] = green[chosen[i]]
        copy_t(peer).start()
        return carry

    lax.fori_loop(0, ND - 1, start_t, 0)
    recv_t[b] = green[chosen[ND - 1]]

    def arrive_b(u, carry):
        pltpu.make_async_copy(green.at[0], recv_d.at[u], sem_rd.at[u]).wait()

        @pl.when(u != b)
        def _():
            pltpu.make_async_copy(green.at[0], recv_t.at[u], sem_rt.at[u]).wait()

        return carry

    def pair_up(pair, carry):
        arrive_b(2 * pair, 0)
        arrive_b(2 * pair + 1, 0)
        even = recv_d[2 * pair].astype(F32)
        other = recv_d[2 * pair + 1].astype(F32)
        direct_re[pair] = jnp.where(left, even, swap(other))
        direct_im[pair] = jnp.where(left, swap(even), other)
        both = recv_t[pl.ds(2 * pair, 2)].astype(F32).reshape(2 * NF, PACK).T
        turned_re[pair, 16 : 16 + NF, :] = pick(both[0:NF], skew)
        turned_im[pair, 16 : 16 + NF, :] = pick(both[NF:PACK], skew)
        return carry

    lax.fori_loop(0, NM // 2, pair_up, 0)

    def copy_o(peer):
        return pltpu.make_async_remote_copy(
            src_ref=send_o.at[peer],
            dst_ref=out.at[source],
            send_sem=sem_so.at[peer],
            recv_sem=sem_ro.at[source],
            device_id=(w, peer),
            device_id_type=MESH,
        )

    def window(i, carry):
        peer = along_blk(i)
        offsets = [transfers[2 * peer + k] for k in range(2)]

        def multiply(step, carry):
            first = pl.multiple_of(step * BAND, BAND)
            band = pl.ds(first, BAND)
            sums = [[jnp.zeros((BAND, PACK), F32)] * 2 for k in range(2)]
            for pair in range(NM // 2):
                near_re = direct_re[pair, band]
                near_im = direct_im[pair, band]
                for k in range(2):
                    far_re = turned_re[pair, pl.ds(offsets[k] + first, BAND), :]
                    far_im = turned_im[pair, pl.ds(offsets[k] + first, BAND), :]
                    sums[k] = [
                        sums[k][0] + (near_re * far_re - near_im * far_im),
                        sums[k][1] + (near_re * far_im + near_im * far_re),
                    ]
            for k in range(2):
                total[2 * k, band] = sums[k][0]
                total[2 * k + 1, band] = sums[k][1]
            return carry

        lax.fori_loop(0, NF // BAND, multiply, 0)
        for k in range(2):
            sum_re, sum_im = [value + swap(value) for value in (total[2 * k], total[2 * k + 1])]
            nu = offsets[k] - NQ // 2
            row = row_of + nu
            col = lane_of + nu
            keep = (row >= 0) & (row < NF) & (col >= 0) & (col < NF)
            result = pick(jnp.where(left, sum_re, sum_im), straight)
            send_o[peer, k] = jnp.where(keep, result, 0.0).astype(BF16)

        @pl.when(i < ND - 1)
        def _():
            copy_o(peer).start()

        return carry

    lax.fori_loop(0, ND, window, 0)
    own_o = pltpu.make_async_copy(send_o.at[b], out.at[source], sem_ro.at[source])
    own_o.start()

    def arrive_o(i, carry):
        pltpu.make_async_copy(send_o.at[i], out.at[i], sem_ro.at[i]).wait()
        return carry

    lax.fori_loop(0, ND, arrive_o, 0)

    def drain(i, carry):
        peer = lax.rem(b + i, ND)
        copy_t(peer).wait_send()
        copy_o(peer).wait_send()
        return carry

    lax.fori_loop(1, ND, drain, 0)

    def drain_d(m, carry):
        @pl.when(jnp.logical_not(is_own(m)))
        def _():
            copy_d(m).wait_send()

        return carry

    lax.fori_loop(0, NM, drain_d, 0)


def spread_out(inverse, blocks, out):
    left = lax.broadcasted_iota(jnp.int32, (NF, PACK), 1) < NF
    for tile in range(NM // 2):
        even = blocks[inverse[2 * tile]].astype(F32)
        other = blocks[inverse[2 * tile + 1]].astype(F32)
        for k in range(2):
            out[0, k, :, tile * 128 : tile * 128 + 128] = jnp.where(left, even[k], swap(other[k]))
            out[1, k, :, tile * 128 : tile * 128 + 128] = jnp.where(left, swap(even[k]), other[k])


def shards(vertex_times, vertex_sites, vertex_matrix, bare_green, transfer_momentum, transfers):
    vmem = pl.BlockSpec(memory_space=pltpu.VMEM)
    smem = pl.BlockSpec(memory_space=pltpu.SMEM)
    here = pl.BlockSpec(memory_space=pl.ANY)
    sems = pltpu.SemaphoreType.DMA((ND,))
    blocks = pltpu.VMEM((ND, NF, PACK), BF16)
    pairs = pltpu.VMEM((NM // 2, NF, PACK), F32)
    padded = pltpu.VMEM((NM // 2, NF + 32, PACK), F32)
    results, inverse = pl.pallas_call(
        kernel,
        out_shape=[
            jax.ShapeDtypeStruct((ND, 2, NF, PACK), BF16),
            jax.ShapeDtypeStruct((NM,), jnp.int32),
        ],
        in_specs=[here] * 6,
        out_specs=[here, smem],
        scratch_shapes=[
            pltpu.VMEM((1, NV), jnp.int32),
            pltpu.VMEM((1, NV), jnp.int32),
            pltpu.VMEM((1, NF, NV), BF16),
            pltpu.VMEM((2, NV), F32),
            pltpu.SMEM((NM,), jnp.int32),
            pltpu.SMEM((NQ,), jnp.int32),
            pltpu.VMEM((2, NF, NV), BF16),
            pltpu.VMEM((NM, PACK, NV), BF16),
            pltpu.VMEM((NV, PACK), F32),
            pltpu.VMEM((NV, PACK), F32),
            pltpu.VMEM((NM, 8, PACK), F32),
            pltpu.SMEM((NM,), jnp.int32),
            blocks,
            pltpu.VMEM((NV, PACK), BF16),
            blocks,
            blocks,
            blocks,
            blocks,
            blocks,
            pairs,
            pairs,
            padded,
            padded,
            pltpu.VMEM((4, NF, PACK), F32),
            pltpu.VMEM((ND, 2, NF, PACK), BF16),
            pltpu.SemaphoreType.DMA((6,)),
        ]
        + [sems] * 8,
        compiler_params=pltpu.CompilerParams(collective_id=0, has_side_effects=True),
    )(vertex_times, vertex_sites, vertex_matrix, bare_green, transfer_momentum, transfers)
    return pl.pallas_call(
        spread_out,
        out_shape=jax.ShapeDtypeStruct((2, 2, NF, NV), F32),
        in_specs=[smem, vmem],
        out_specs=vmem,
    )(inverse, results)


def solution(mesh):
    return jax.shard_map(
        shards,
        mesh=mesh,
        in_specs=(P("blk", None), P("blk", None), P("blk", "walk", None), P(), P(), P()),
        out_specs=P(None, "blk", "walk", None),
        check_vma=False,
    )
```

```python
import math

import jax
import jax.numpy as jnp
from jax import lax
from jax.experimental import pallas as pl
from jax.experimental.pallas import tpu as pltpu
from jax.sharding import PartitionSpec as P

NM = 16
NF = 64
NV = 1024
NT = 4096
NQ = 32
SIDE = 4
ND = 16
PACK = 2 * NF
TURN = 8 * NT
QUARTER = TURN // 4
BAND = 16
MESH = pl.DeviceIdType.MESH
F32 = jnp.float32
BF16 = jnp.bfloat16


def sincos(phase):
    quadrant = (phase + QUARTER // 2) >> 13
    angle = (phase - (quadrant << 13)).astype(F32) * (2.0 * math.pi / TURN)
    square = angle * angle
    sine = angle * (
        1.0 + square * (-1.0 / 6 + square * (1.0 / 120 + square * (-1.0 / 5040 + square * (1.0 / 362880))))
    )
    cosine = 1.0 + square * (
        -0.5 + square * (1.0 / 24 + square * (-1.0 / 720 + square * (1.0 / 40320 - square * (1.0 / 3628800))))
    )
    odd = (quadrant & 1) == 1
    sign = (1 - (quadrant & 2)).astype(F32)
    return jnp.where(odd, -sine, cosine) * sign, jnp.where(odd, cosine, sine) * sign


def pick(value, lanes):
    return jnp.take_along_axis(value, lanes, axis=1)


def swap(value):
    return pltpu.roll(value, NF, 1)


def kernel(
    times_in,
    sites_in,
    matrix_in,
    bare_in,
    shift_in,
    transfers_in,
    out,
    inverse,
    times,
    sites,
    matrix,
    bare,
    shift,
    transfers,
    factor,
    base,
    partial,
    projected,
    table,
    outer_re,
    outer_im,
    chosen,
    send_a,
    recv_a,
    held,
    green,
    send_d,
    send_t,
    recv_d,
    recv_t,
    direct_re,
    direct_im,
    turned_re,
    turned_im,
    total,
    send_o,
    sem_in,
    sem_sa,
    sem_ra,
    sem_sd,
    sem_rd,
    sem_st,
    sem_rt,
    sem_so,
    sem_ro,
):
    w = lax.axis_index("walk")
    b = lax.axis_index("blk")
    source = (b - w) & (ND - 1)
    alone = source == w

    def along_walk(i):
        z = (w >> 1) + (4, 3, 5, 2, 6, 1, 7, 0)[i // 2]
        return ((z & 7) << 1) + ((w + i + 1) & 1)

    def along_blk(i):
        y = (b >> 1) + (2, 1, 3, 0)[i // 4]
        x = (b >> 3) + 1 - (i % 4) // 2
        return ((x & 1) << 3) + ((y & 3) << 1) + ((b + i + 1) & 1)

    barrier = pltpu.get_barrier_semaphore()

    incoming = [
        pltpu.make_async_copy(held, here, sem_in.at[k])
        for k, (held, here) in enumerate(
            (
                (times_in, times),
                (sites_in, sites),
                (matrix_in, matrix),
                (bare_in, bare),
                (shift_in, shift),
                (transfers_in, transfers),
            )
        )
    ]
    for copy in incoming:
        copy.start()
    for i in range(ND - 1):
        pl.semaphore_signal(barrier, inc=1, device_id=(along_walk(i), b), device_id_type=MESH)
        pl.semaphore_signal(barrier, inc=1, device_id=(w, along_blk(i)), device_id_type=MESH)
    for copy in incoming:
        copy.wait()

    step = lax.broadcasted_iota(jnp.int32, (16, NV), 0)
    step = jnp.where(step < 8, 64 * step, 8 * (step - 8) + 4 * (1 - NF))
    cosine, sine = sincos((step * times[...]) & (TURN - 1))
    factor[0] = cosine
    factor[1] = sine
    fine_cos = factor[0, 8:16, :]
    fine_sin = factor[1, 8:16, :]
    for g in range(0, 8, 2):
        coarse = [(factor[0, g + k : g + k + 1, :], factor[1, g + k : g + k + 1, :]) for k in range(2)]
        base[8 * g : 8 * g + 16, :] = jnp.concatenate(
            [c * fine_cos - n * fine_sin for c, n in coarse], axis=0
        ).astype(BF16)
        base[NF + 8 * g : NF + 8 * g + 16, :] = jnp.concatenate(
            [n * fine_cos + c * fine_sin for c, n in coarse], axis=0
        ).astype(BF16)

    left = lax.broadcasted_iota(jnp.int32, (NF, PACK), 1) < NF
    row_of = lax.broadcasted_iota(jnp.int32, (NF, PACK), 0)
    whole_lane = lax.broadcasted_iota(jnp.int32, (NF, PACK), 1)
    lane_of = whole_lane & (NF - 1)
    skew = (whole_lane & NF) | ((whole_lane + row_of) & (NF - 1))
    straight = (whole_lane & NF) | ((whole_lane - row_of) & (NF - 1))
    minus_left = jnp.where(left, -1.0, 1.0)
    scale = NV ** (-0.5)

    def quarter(block):
        return -minus_left * swap(block)

    def turns(blocks):
        even, odd = blocks[0] + blocks[2], blocks[1] + blocks[3]
        apart, turned = blocks[0] - blocks[2], quarter(blocks[1] - blocks[3])
        return even + odd, apart + turned, even - odd, apart - turned

    for x in range(SIDE):
        rows = []
        for y in range(SIDE):
            here = jnp.where(sites[...] == SIDE * x + y, 1.0, 0.0)
            rows.append(matrix[0] * jnp.broadcast_to(here, (NF, NV)).astype(BF16))
        block = lax.dot_general(
            jnp.concatenate(rows, axis=0), base[...], (((1,), (1,)), ((), ())), preferred_element_type=F32
        )
        for y, value in enumerate(turns([block[NF * y : NF * y + NF] for y in range(SIDE)])):
            partial[SIDE * x + y] = value
    for y in range(SIDE):
        for x, value in enumerate(turns([partial[SIDE * x + y] for x in range(SIDE)])):
            m = SIDE * x + y
            piece_re = bare[0:1, m * NF : m * NF + NF] * scale
            piece_im = bare[1:2, m * NF : m * NF + NF] * scale
            value = value * jnp.concatenate([piece_re, -piece_re], axis=1) + swap(value) * jnp.concatenate(
                [piece_im, piece_im], axis=1
            )
            projected[m] = value.astype(BF16)
    for i in range(ND):
        send_a[i] = projected[shift[along_walk(i)]]

    pl.semaphore_wait(barrier, 2 * ND - 2)

    def rows_from(peer):
        return recv_a.at[pl.ds(pl.multiple_of(peer * NF, NF), NF)]

    def copy_a(i):
        peer = along_walk(i)
        return pltpu.make_async_remote_copy(
            src_ref=send_a.at[i],
            dst_ref=rows_from(w),
            send_sem=sem_sa.at[i],
            recv_sem=sem_ra.at[w],
            device_id=(peer, b),
            device_id_type=MESH,
        )

    for i in range(ND - 1):
        copy_a(i).start()
    recv_a[pl.ds(pl.multiple_of(w * NF, NF), NF), :] = send_a[ND - 1]

    def rotate(m, carry):
        turn = ((m >> 2) * (sites[...] >> 2) + (m & 3) * (sites[...] & 3)) & 3
        sign = (1 - (turn & 2)).astype(F32)
        odd = (turn & 1).astype(F32)
        along = jnp.broadcast_to((1.0 - odd) * sign, (NF, NV)).astype(BF16)
        across = jnp.broadcast_to(odd * sign, (NF, NV)).astype(BF16)
        cosine = base[0:NF]
        sine = base[NF:PACK]
        table[m, 0:NF, :] = cosine * along + sine * across
        table[m, NF:PACK, :] = sine * along - cosine * across
        return carry

    lax.fori_loop(0, NM, rotate, 0)

    for part, target in ((0, outer_re), (1, outer_im)):
        for tile in range(NV // 128):
            row = jnp.broadcast_to(bare[part : part + 1, tile * 128 : tile * 128 + 128], (128, 128))
            column = row.T
            if part == 1:
                column = jnp.where(lax.broadcasted_iota(jnp.int32, (128, 128), 1) < NF, -column, column)
            target[tile * 128 : tile * 128 + 128, :] = column

    for m in range(NM):
        position = jnp.int32(0)
        for i in range(1, NM):
            position = jnp.where(shift[i] == m, i, position)
        inverse[m] = position

    for target in (turned_re, turned_im):
        for pair in range(NM // 2):
            target[pair, 0:16, :] = jnp.zeros((16, 128), F32)
            target[pair, 80:96, :] = jnp.zeros((16, 128), F32)

    mine = shift[w]
    for i in range(ND):
        chosen[i] = shift[shift[(along_blk(i) - w) & (ND - 1)]]

    for i in range(ND - 1):
        peer = along_walk(i)
        pltpu.make_async_copy(send_a.at[i], rows_from(peer), sem_ra.at[peer]).wait()
        copy_a(i).wait_send()

    def copy_d(m):
        return pltpu.make_async_remote_copy(
            src_ref=send_d.at[m],
            dst_ref=recv_d.at[b],
            send_sem=sem_sd.at[m],
            recv_sem=sem_rd.at[b],
            device_id=(m, (w + m) & (ND - 1)),
            device_id_type=MESH,
        )

    def own_d(m):
        return pltpu.make_async_copy(send_d.at[m], recv_d.at[b], sem_rd.at[b])

    def is_own(m):
        return jnp.logical_and(alone, m == w)

    diagonal = jnp.where(jnp.logical_and(left, row_of == lane_of), 1.0, 0.0)

    def assemble(group):
        raw = held.at[group % 2]
        for k in range(4):
            m = 4 * group + k
            part = raw[k * PACK : k * PACK + NF, :] + swap(raw[k * PACK + NF : (k + 1) * PACK, :]) * minus_left
            part = part + diagonal * (mine == m).astype(F32)
            rows = slice(m * NF, m * NF + NF)
            value = outer_re[rows, :] * part + outer_im[rows, :] * swap(part)
            green[m] = value.astype(BF16)
            send_d[m] = pick(value, skew).astype(BF16)

    for group in range(NM // 4 + 1):
        if group < NM // 4:
            held[group % 2] = jnp.dot(
                table[4 * group : 4 * group + 4].reshape(4 * PACK, NV), recv_a[...], preferred_element_type=F32
            )
        if group > 0:
            assemble(group - 1)
            for k in range(4):
                m = 4 * (group - 1) + k

                @pl.when(jnp.logical_not(is_own(m)))
                def _():
                    copy_d(m).start()

    @pl.when(alone)
    def _():
        own_d(w).start()

    def copy_t(i):
        return pltpu.make_async_remote_copy(
            src_ref=send_t.at[i],
            dst_ref=recv_t.at[b],
            send_sem=sem_st.at[i],
            recv_sem=sem_rt.at[b],
            device_id=(w, along_blk(i)),
            device_id_type=MESH,
        )

    for i in range(ND - 1):
        send_t[i] = green[chosen[i]]
        copy_t(i).start()
    recv_t[b] = green[chosen[ND - 1]]

    def arrive_b(u, carry):
        pltpu.make_async_copy(green.at[0], recv_d.at[u], sem_rd.at[u]).wait()

        @pl.when(u != b)
        def _():
            pltpu.make_async_copy(green.at[0], recv_t.at[u], sem_rt.at[u]).wait()

        return carry

    def pair_up(pair, carry):
        arrive_b(2 * pair, 0)
        arrive_b(2 * pair + 1, 0)
        even = recv_d[2 * pair].astype(F32)
        other = recv_d[2 * pair + 1].astype(F32)
        direct_re[pair] = jnp.where(left, even, swap(other))
        direct_im[pair] = jnp.where(left, swap(even), other)
        both = recv_t[pl.ds(2 * pair, 2)].astype(F32).reshape(2 * NF, PACK).T
        turned_re[pair, 16 : 16 + NF, :] = pick(both[0:NF], skew)
        turned_im[pair, 16 : 16 + NF, :] = pick(both[NF:PACK], skew)
        return carry

    lax.fori_loop(0, NM // 2, pair_up, 0)

    def peer_o(i):
        step = i >> 2
        y = (b >> 1) + 2 - step + 3 * (step >> 1) - 2 * (step & (step >> 1))
        x = (b >> 3) + 1 - ((i & 3) >> 1)
        return ((x & 1) << 3) + ((y & 3) << 1) + ((b + i + 1) & 1)

    def copy_o(i):
        return pltpu.make_async_remote_copy(
            src_ref=send_o.at[i],
            dst_ref=out.at[source],
            send_sem=sem_so.at[i],
            recv_sem=sem_ro.at[source],
            device_id=(w, peer_o(i)),
            device_id_type=MESH,
        )

    def window(i, carry):
        peer = peer_o(i)
        offsets = [transfers[2 * peer + k] for k in range(2)]

        def multiply(step, carry):
            first = pl.multiple_of(step * BAND, BAND)
            band = pl.ds(first, BAND)
            sums = [[jnp.zeros((BAND, PACK), F32)] * 2 for k in range(2)]
            for pair in range(NM // 2):
                near_re = direct_re[pair, band]
                near_im = direct_im[pair, band]
                for k in range(2):
                    far_re = turned_re[pair, pl.ds(offsets[k] + first, BAND), :]
                    far_im = turned_im[pair, pl.ds(offsets[k] + first, BAND), :]
                    sums[k] = [
                        sums[k][0] + (near_re * far_re - near_im * far_im),
                        sums[k][1] + (near_re * far_im + near_im * far_re),
                    ]
            for k in range(2):
                total[2 * k, band] = sums[k][0]
                total[2 * k + 1, band] = sums[k][1]
            return carry

        lax.fori_loop(0, NF // BAND, multiply, 0)
        for k in range(2):
            sum_re, sum_im = [value + swap(value) for value in (total[2 * k], total[2 * k + 1])]
            nu = offsets[k] - NQ // 2
            row = row_of + nu
            col = lane_of + nu
            keep = (row >= 0) & (row < NF) & (col >= 0) & (col < NF)
            result = pick(jnp.where(left, sum_re, sum_im), straight)
            send_o[i, k] = jnp.where(keep, result, 0.0).astype(BF16)

        @pl.when(i < ND - 1)
        def _():
            copy_o(i).start()

        return carry

    lax.fori_loop(0, ND, window, 0)
    own_o = pltpu.make_async_copy(send_o.at[ND - 1], out.at[source], sem_ro.at[source])
    own_o.start()

    def arrive_o(i, carry):
        pltpu.make_async_copy(send_o.at[i], out.at[i], sem_ro.at[i]).wait()
        return carry

    lax.fori_loop(0, ND, arrive_o, 0)

    for i in range(ND - 1):
        copy_t(i).wait_send()
        copy_o(i).wait_send()

    def drain_d(m, carry):
        @pl.when(jnp.logical_not(is_own(m)))
        def _():
            copy_d(m).wait_send()

        return carry

    lax.fori_loop(0, NM, drain_d, 0)


def spread_out(inverse, blocks, out):
    left = lax.broadcasted_iota(jnp.int32, (NF, PACK), 1) < NF
    for tile in range(NM // 2):
        even = blocks[inverse[2 * tile]].astype(F32)
        other = blocks[inverse[2 * tile + 1]].astype(F32)
        for k in range(2):
            out[0, k, :, tile * 128 : tile * 128 + 128] = jnp.where(left, even[k], swap(other[k]))
            out[1, k, :, tile * 128 : tile * 128 + 128] = jnp.where(left, swap(even[k]), other[k])


def shards(vertex_times, vertex_sites, vertex_matrix, bare_green, transfer_momentum, transfers):
    vmem = pl.BlockSpec(memory_space=pltpu.VMEM)
    smem = pl.BlockSpec(memory_space=pltpu.SMEM)
    here = pl.BlockSpec(memory_space=pl.ANY)
    sems = pltpu.SemaphoreType.DMA((ND,))
    blocks = pltpu.VMEM((ND, NF, PACK), BF16)
    pairs = pltpu.VMEM((NM // 2, NF, PACK), F32)
    padded = pltpu.VMEM((NM // 2, NF + 32, PACK), F32)
    results, inverse = pl.pallas_call(
        kernel,
        out_shape=[
            jax.ShapeDtypeStruct((ND, 2, NF, PACK), BF16),
            jax.ShapeDtypeStruct((NM,), jnp.int32),
        ],
        in_specs=[here] * 6,
        out_specs=[here, smem],
        scratch_shapes=[
            pltpu.VMEM((1, NV), jnp.int32),
            pltpu.VMEM((1, NV), jnp.int32),
            pltpu.VMEM((1, NF, NV), BF16),
            pltpu.VMEM((2, NV), F32),
            pltpu.SMEM((NM,), jnp.int32),
            pltpu.SMEM((NQ,), jnp.int32),
            pltpu.VMEM((2, 16, NV), F32),
            pltpu.VMEM((PACK, NV), BF16),
            pltpu.VMEM((NM, NF, PACK), F32),
            blocks,
            pltpu.VMEM((NM, PACK, NV), BF16),
            pltpu.VMEM((NV, PACK), F32),
            pltpu.VMEM((NV, PACK), F32),
            pltpu.SMEM((NM,), jnp.int32),
            blocks,
            pltpu.VMEM((NV, PACK), BF16),
            pltpu.VMEM((2, 4 * PACK, PACK), F32),
            blocks,
            blocks,
            blocks,
            blocks,
            blocks,
            pairs,
            pairs,
            padded,
            padded,
            pltpu.VMEM((4, NF, PACK), F32),
            pltpu.VMEM((ND, 2, NF, PACK), BF16),
            pltpu.SemaphoreType.DMA((6,)),
        ]
        + [sems] * 8,
        compiler_params=pltpu.CompilerParams(collective_id=0, has_side_effects=True),
    )(vertex_times, vertex_sites, vertex_matrix, bare_green, transfer_momentum, transfers)
    return pl.pallas_call(
        spread_out,
        out_shape=jax.ShapeDtypeStruct((2, 2, NF, NV), F32),
        in_specs=[smem, vmem],
        out_specs=vmem,
    )(inverse, results)


def solution(mesh):
    return jax.shard_map(
        shards,
        mesh=mesh,
        in_specs=(P("blk", None), P("blk", None), P("blk", "walk", None), P(), P(), P()),
        out_specs=P(None, "blk", "walk", None),
        check_vma=False,
    )
```

```python
import math

import jax
import jax.numpy as jnp
from jax import lax
from jax.experimental import pallas as pl
from jax.experimental.pallas import tpu as pltpu
from jax.sharding import PartitionSpec as P

NM = 16
NF = 64
NV = 1024
NT = 4096
NQ = 32
SIDE = 4
ND = 16
PACK = 2 * NF
TURN = 8 * NT
QUARTER = TURN // 4
BAND = 16
MESH = pl.DeviceIdType.MESH
F32 = jnp.float32
BF16 = jnp.bfloat16


def sincos(phase):
    quadrant = (phase + QUARTER // 2) >> 13
    angle = (phase - (quadrant << 13)).astype(F32) * (2.0 * math.pi / TURN)
    square = angle * angle
    sine = angle * (
        1.0 + square * (-1.0 / 6 + square * (1.0 / 120 + square * (-1.0 / 5040 + square * (1.0 / 362880))))
    )
    cosine = 1.0 + square * (
        -0.5 + square * (1.0 / 24 + square * (-1.0 / 720 + square * (1.0 / 40320 - square * (1.0 / 3628800))))
    )
    odd = (quadrant & 1) == 1
    sign = (1 - (quadrant & 2)).astype(F32)
    return jnp.where(odd, -sine, cosine) * sign, jnp.where(odd, cosine, sine) * sign


def pick(value, lanes):
    return jnp.take_along_axis(value, lanes, axis=1)


def swap(value):
    return pltpu.roll(value, NF, 1)


def kernel(
    times_in,
    sites_in,
    matrix_in,
    bare_in,
    shift_in,
    transfers_in,
    out,
    inverse,
    times,
    sites,
    matrix,
    bare,
    shift,
    transfers,
    factor,
    base,
    partial,
    column,
    projected,
    table,
    outer_re,
    outer_im,
    chosen,
    send_a,
    recv_a,
    held,
    green,
    send_d,
    send_t,
    recv_d,
    recv_t,
    direct_re,
    direct_im,
    turned_re,
    turned_im,
    total,
    send_o,
    sem_in,
    sem_sa,
    sem_ra,
    sem_sd,
    sem_rd,
    sem_st,
    sem_rt,
    sem_so,
    sem_ro,
):
    w = lax.axis_index("walk")
    b = lax.axis_index("blk")
    source = (b - w) & (ND - 1)
    alone = source == w

    def along_walk(i):
        z = (w >> 1) + (4, 3, 5, 2, 6, 1, 7, 0)[i // 2]
        return ((z & 7) << 1) + ((w + i + 1) & 1)

    def along_blk(i):
        y = (b >> 1) + (2, 1, 3, 0)[i // 4]
        x = (b >> 3) + 1 - (i % 4) // 2
        return ((x & 1) << 3) + ((y & 3) << 1) + ((b + i + 1) & 1)

    barrier = pltpu.get_barrier_semaphore()

    incoming = [
        pltpu.make_async_copy(held, here, sem_in.at[k])
        for k, (held, here) in enumerate(
            (
                (times_in, times),
                (sites_in, sites),
                (matrix_in, matrix),
                (bare_in, bare),
                (shift_in, shift),
                (transfers_in, transfers),
            )
        )
    ]
    for copy in incoming:
        copy.start()
    for i in range(ND - 1):
        pl.semaphore_signal(barrier, inc=1, device_id=(along_walk(i), b), device_id_type=MESH)
        pl.semaphore_signal(barrier, inc=1, device_id=(w, along_blk(i)), device_id_type=MESH)
    for copy in incoming:
        copy.wait()

    step = lax.broadcasted_iota(jnp.int32, (16, NV), 0)
    step = jnp.where(step < 8, 64 * step, 8 * (step - 8) + 4 * (1 - NF))
    cosine, sine = sincos((step * times[...]) & (TURN - 1))
    factor[0] = cosine
    factor[1] = sine
    fine_cos = factor[0, 8:16, :]
    fine_sin = factor[1, 8:16, :]
    for g in range(0, 8, 2):
        coarse = [(factor[0, g + k : g + k + 1, :], factor[1, g + k : g + k + 1, :]) for k in range(2)]
        base[8 * g : 8 * g + 16, :] = jnp.concatenate(
            [c * fine_cos - n * fine_sin for c, n in coarse], axis=0
        ).astype(BF16)
        base[NF + 8 * g : NF + 8 * g + 16, :] = jnp.concatenate(
            [n * fine_cos + c * fine_sin for c, n in coarse], axis=0
        ).astype(BF16)

    left = lax.broadcasted_iota(jnp.int32, (NF, PACK), 1) < NF
    row_of = lax.broadcasted_iota(jnp.int32, (NF, PACK), 0)
    whole_lane = lax.broadcasted_iota(jnp.int32, (NF, PACK), 1)
    lane_of = whole_lane & (NF - 1)
    skew = (whole_lane & NF) | ((whole_lane + row_of) & (NF - 1))
    straight = (whole_lane & NF) | ((whole_lane - row_of) & (NF - 1))
    minus_left = jnp.where(left, -1.0, 1.0)
    scale = NV ** (-0.5)

    def quarter(block):
        return -minus_left * swap(block)

    def turns(blocks):
        even, odd = blocks[0] + blocks[2], blocks[1] + blocks[3]
        apart, turned = blocks[0] - blocks[2], quarter(blocks[1] - blocks[3])
        return even + odd, apart + turned, even - odd, apart - turned

    for m in range(NM):
        piece_re = bare[0:1, m * NF : m * NF + NF] * scale
        piece_im = bare[1:2, m * NF : m * NF + NF] * scale
        column[m, 0:1, :] = jnp.concatenate([piece_re, -piece_re], axis=1)
        column[m, 1:2, :] = jnp.concatenate([piece_im, piece_im], axis=1)

    for x in range(SIDE):
        rows = []
        for y in range(SIDE):
            here = jnp.where(sites[...] == SIDE * x + y, 1.0, 0.0)
            rows.append(matrix[0] * jnp.broadcast_to(here, (NF, NV)).astype(BF16))
        block = lax.dot_general(
            jnp.concatenate(rows, axis=0), base[...], (((1,), (1,)), ((), ())), preferred_element_type=F32
        )
        for y, value in enumerate(turns([block[NF * y : NF * y + NF] for y in range(SIDE)])):
            partial[SIDE * x + y] = value
    def join(y, carry):
        for x, value in enumerate(turns([partial[SIDE * x + y] for x in range(SIDE)])):
            factors = column[SIDE * x + y]
            projected[SIDE * x + y] = (value * factors[0:1] + swap(value) * factors[1:2]).astype(BF16)
        return carry

    lax.fori_loop(0, SIDE, join, 0)
    for i in range(ND):
        send_a[i] = projected[shift[along_walk(i)]]

    pl.semaphore_wait(barrier, 2 * ND - 2)

    def rows_from(peer):
        return recv_a.at[pl.ds(pl.multiple_of(peer * NF, NF), NF)]

    def copy_a(i):
        peer = along_walk(i)
        return pltpu.make_async_remote_copy(
            src_ref=send_a.at[i],
            dst_ref=rows_from(w),
            send_sem=sem_sa.at[i],
            recv_sem=sem_ra.at[w],
            device_id=(peer, b),
            device_id_type=MESH,
        )

    for i in range(ND - 1):
        copy_a(i).start()
    recv_a[pl.ds(pl.multiple_of(w * NF, NF), NF), :] = send_a[ND - 1]

    def rotate(m, carry):
        turn = ((m >> 2) * (sites[...] >> 2) + (m & 3) * (sites[...] & 3)) & 3
        sign = (1 - (turn & 2)).astype(F32)
        odd = (turn & 1).astype(F32)
        along = jnp.broadcast_to((1.0 - odd) * sign, (NF, NV)).astype(BF16)
        across = jnp.broadcast_to(odd * sign, (NF, NV)).astype(BF16)
        cosine = base[0:NF]
        sine = base[NF:PACK]
        table[m, 0:NF, :] = cosine * along + sine * across
        table[m, NF:PACK, :] = sine * along - cosine * across
        return carry

    lax.fori_loop(0, NM, rotate, 0)

    for part, target in ((0, outer_re), (1, outer_im)):
        for tile in range(NV // 128):
            row = jnp.broadcast_to(bare[part : part + 1, tile * 128 : tile * 128 + 128], (128, 128))
            column = row.T
            if part == 1:
                column = jnp.where(lax.broadcasted_iota(jnp.int32, (128, 128), 1) < NF, -column, column)
            target[tile * 128 : tile * 128 + 128, :] = column

    for m in range(NM):
        position = jnp.int32(0)
        for i in range(1, NM):
            position = jnp.where(shift[i] == m, i, position)
        inverse[m] = position

    for target in (turned_re, turned_im):
        for pair in range(NM // 2):
            target[pair, 0:16, :] = jnp.zeros((16, 128), F32)
            target[pair, 80:96, :] = jnp.zeros((16, 128), F32)

    mine = shift[w]
    for i in range(ND):
        chosen[i] = shift[shift[(along_blk(i) - w) & (ND - 1)]]

    for i in range(ND - 1):
        peer = along_walk(i)
        pltpu.make_async_copy(send_a.at[i], rows_from(peer), sem_ra.at[peer]).wait()
        copy_a(i).wait_send()

    def copy_d(m):
        return pltpu.make_async_remote_copy(
            src_ref=send_d.at[m],
            dst_ref=recv_d.at[b],
            send_sem=sem_sd.at[m],
            recv_sem=sem_rd.at[b],
            device_id=(m, (w + m) & (ND - 1)),
            device_id_type=MESH,
        )

    def own_d(m):
        return pltpu.make_async_copy(send_d.at[m], recv_d.at[b], sem_rd.at[b])

    def is_own(m):
        return jnp.logical_and(alone, m == w)

    diagonal = jnp.where(jnp.logical_and(left, row_of == lane_of), 1.0, 0.0)

    def assemble(group):
        raw = held.at[group % 2]
        for k in range(4):
            m = 4 * group + k
            part = raw[k * PACK : k * PACK + NF, :] + swap(raw[k * PACK + NF : (k + 1) * PACK, :]) * minus_left
            part = part + diagonal * (mine == m).astype(F32)
            rows = slice(m * NF, m * NF + NF)
            value = outer_re[rows, :] * part + outer_im[rows, :] * swap(part)
            green[m] = value.astype(BF16)
            send_d[m] = pick(value, skew).astype(BF16)

    for group in range(NM // 4 + 1):
        if group < NM // 4:
            held[group % 2] = jnp.dot(
                table[4 * group : 4 * group + 4].reshape(4 * PACK, NV), recv_a[...], preferred_element_type=F32
            )
        if group > 0:
            assemble(group - 1)
            for k in range(4):
                m = 4 * (group - 1) + k

                @pl.when(jnp.logical_not(is_own(m)))
                def _():
                    copy_d(m).start()

    @pl.when(alone)
    def _():
        own_d(w).start()

    def copy_t(i):
        return pltpu.make_async_remote_copy(
            src_ref=send_t.at[i],
            dst_ref=recv_t.at[b],
            send_sem=sem_st.at[i],
            recv_sem=sem_rt.at[b],
            device_id=(w, along_blk(i)),
            device_id_type=MESH,
        )

    for i in range(ND - 1):
        send_t[i] = green[chosen[i]]
        copy_t(i).start()
    recv_t[b] = green[chosen[ND - 1]]

    def arrive_b(u, carry):
        pltpu.make_async_copy(green.at[0], recv_d.at[u], sem_rd.at[u]).wait()

        @pl.when(u != b)
        def _():
            pltpu.make_async_copy(green.at[0], recv_t.at[u], sem_rt.at[u]).wait()

        return carry

    def pair_up(step, carry):
        for u in range(16):
            arrive_b(16 * step + u, 0)
        for k in range(8):
            pair = 8 * step + k
            even = recv_d[2 * pair].astype(F32)
            other = recv_d[2 * pair + 1].astype(F32)
            direct_re[pair] = jnp.where(left, even, swap(other))
            direct_im[pair] = jnp.where(left, swap(even), other)
            both = recv_t[pl.ds(2 * pair, 2)].astype(F32).reshape(2 * NF, PACK).T
            turned_re[pair, 16 : 16 + NF, :] = pick(both[0:NF], skew)
            turned_im[pair, 16 : 16 + NF, :] = pick(both[NF:PACK], skew)
        return carry

    lax.fori_loop(0, NM // 16, pair_up, 0)

    def peer_o(i):
        step = i >> 2
        y = (b >> 1) + 2 - step + 3 * (step >> 1) - 2 * (step & (step >> 1))
        x = (b >> 3) + 1 - ((i & 3) >> 1)
        return ((x & 1) << 3) + ((y & 3) << 1) + ((b + i + 1) & 1)

    def copy_o(i):
        return pltpu.make_async_remote_copy(
            src_ref=send_o.at[i],
            dst_ref=out.at[source],
            send_sem=sem_so.at[i],
            recv_sem=sem_ro.at[source],
            device_id=(w, peer_o(i)),
            device_id_type=MESH,
        )

    def window(i, carry):
        peer = peer_o(i)
        offsets = [transfers[2 * peer + k] for k in range(2)]

        def multiply(step, carry):
            first = pl.multiple_of(step * BAND, BAND)
            band = pl.ds(first, BAND)
            sums = [[jnp.zeros((BAND, PACK), F32)] * 2 for k in range(2)]
            for pair in range(NM // 2):
                near_re = direct_re[pair, band]
                near_im = direct_im[pair, band]
                for k in range(2):
                    far_re = turned_re[pair, pl.ds(offsets[k] + first, BAND), :]
                    far_im = turned_im[pair, pl.ds(offsets[k] + first, BAND), :]
                    sums[k] = [
                        sums[k][0] + (near_re * far_re - near_im * far_im),
                        sums[k][1] + (near_re * far_im + near_im * far_re),
                    ]
            for k in range(2):
                total[2 * k, band] = sums[k][0]
                total[2 * k + 1, band] = sums[k][1]
            return carry

        lax.fori_loop(0, NF // BAND, multiply, 0)
        for k in range(2):
            sum_re, sum_im = [value + swap(value) for value in (total[2 * k], total[2 * k + 1])]
            nu = offsets[k] - NQ // 2
            row = row_of + nu
            col = lane_of + nu
            keep = (row >= 0) & (row < NF) & (col >= 0) & (col < NF)
            result = pick(jnp.where(left, sum_re, sum_im), straight)
            send_o[i, k] = jnp.where(keep, result, 0.0).astype(BF16)

        @pl.when(i < ND - 1)
        def _():
            copy_o(i).start()

        return carry

    lax.fori_loop(0, ND, window, 0)
    own_o = pltpu.make_async_copy(send_o.at[ND - 1], out.at[source], sem_ro.at[source])
    own_o.start()

    def arrive_o(i, carry):
        pltpu.make_async_copy(send_o.at[i], out.at[i], sem_ro.at[i]).wait()
        return carry

    lax.fori_loop(0, ND, arrive_o, 0)

    for i in range(ND - 1):
        copy_t(i).wait_send()
        copy_o(i).wait_send()

    def drain_d(m, carry):
        @pl.when(jnp.logical_not(is_own(m)))
        def _():
            copy_d(m).wait_send()

        return carry

    lax.fori_loop(0, NM, drain_d, 0)


def spread_out(inverse, blocks, out):
    left = lax.broadcasted_iota(jnp.int32, (NF, PACK), 1) < NF
    for tile in range(NM // 2):
        even = blocks[inverse[2 * tile]].astype(F32)
        other = blocks[inverse[2 * tile + 1]].astype(F32)
        for k in range(2):
            out[0, k, :, tile * 128 : tile * 128 + 128] = jnp.where(left, even[k], swap(other[k]))
            out[1, k, :, tile * 128 : tile * 128 + 128] = jnp.where(left, swap(even[k]), other[k])


def shards(vertex_times, vertex_sites, vertex_matrix, bare_green, transfer_momentum, transfers):
    vmem = pl.BlockSpec(memory_space=pltpu.VMEM)
    smem = pl.BlockSpec(memory_space=pltpu.SMEM)
    here = pl.BlockSpec(memory_space=pl.ANY)
    sems = pltpu.SemaphoreType.DMA((ND,))
    blocks = pltpu.VMEM((ND, NF, PACK), BF16)
    pairs = pltpu.VMEM((NM // 2, NF, PACK), F32)
    padded = pltpu.VMEM((NM // 2, NF + 32, PACK), F32)
    results, inverse = pl.pallas_call(
        kernel,
        out_shape=[
            jax.ShapeDtypeStruct((ND, 2, NF, PACK), BF16),
            jax.ShapeDtypeStruct((NM,), jnp.int32),
        ],
        in_specs=[pl.BlockSpec(memory_space=pltpu.HBM)] * 6,
        out_specs=[here, smem],
        scratch_shapes=[
            pltpu.VMEM((1, NV), jnp.int32),
            pltpu.VMEM((1, NV), jnp.int32),
            pltpu.VMEM((1, NF, NV), BF16),
            pltpu.VMEM((2, NV), F32),
            pltpu.SMEM((NM,), jnp.int32),
            pltpu.SMEM((NQ,), jnp.int32),
            pltpu.VMEM((2, 16, NV), F32),
            pltpu.VMEM((PACK, NV), BF16),
            pltpu.VMEM((NM, NF, PACK), F32),
            pltpu.VMEM((NM, 8, PACK), F32),
            blocks,
            pltpu.VMEM((NM, PACK, NV), BF16),
            pltpu.VMEM((NV, PACK), F32),
            pltpu.VMEM((NV, PACK), F32),
            pltpu.SMEM((NM,), jnp.int32),
            blocks,
            pltpu.VMEM((NV, PACK), BF16),
            pltpu.VMEM((2, 4 * PACK, PACK), F32),
            blocks,
            blocks,
            blocks,
            blocks,
            blocks,
            pairs,
            pairs,
            padded,
            padded,
            pltpu.VMEM((4, NF, PACK), F32),
            pltpu.VMEM((ND, 2, NF, PACK), BF16),
            pltpu.SemaphoreType.DMA((6,)),
        ]
        + [sems] * 8,
        compiler_params=pltpu.CompilerParams(collective_id=0, has_side_effects=True, vmem_limit_bytes=24 * 2**20),
    )(*[pltpu.with_memory_space_constraint(a, pltpu.HBM) for a in (vertex_times, vertex_sites, vertex_matrix, bare_green, transfer_momentum, transfers)])
    return pl.pallas_call(
        spread_out,
        out_shape=jax.ShapeDtypeStruct((2, 2, NF, NV), F32),
        in_specs=[smem, vmem],
        out_specs=vmem,
        compiler_params=pltpu.CompilerParams(vmem_limit_bytes=16 * 2**20),
    )(inverse, results)


def solution(mesh):
    return jax.shard_map(
        shards,
        mesh=mesh,
        in_specs=(P("blk", None), P("blk", None), P("blk", "walk", None), P(), P(), P()),
        out_specs=P(None, "blk", "walk", None),
        check_vma=False,
    )
```

```python
import math

import jax
import jax.numpy as jnp
from jax import lax
from jax.experimental import pallas as pl
from jax.experimental.pallas import tpu as pltpu
from jax.sharding import PartitionSpec as P

NM = 16
NF = 64
NV = 1024
NT = 4096
NQ = 32
SIDE = 4
ND = 16
PACK = 2 * NF
TURN = 8 * NT
QUARTER = TURN // 4
BAND = 16
MESH = pl.DeviceIdType.MESH
F32 = jnp.float32
BF16 = jnp.bfloat16


def sincos(phase):
    quadrant = (phase + QUARTER // 2) >> 13
    angle = (phase - (quadrant << 13)).astype(F32) * (2.0 * math.pi / TURN)
    square = angle * angle
    sine = angle * (
        1.0 + square * (-1.0 / 6 + square * (1.0 / 120 + square * (-1.0 / 5040 + square * (1.0 / 362880))))
    )
    cosine = 1.0 + square * (
        -0.5 + square * (1.0 / 24 + square * (-1.0 / 720 + square * (1.0 / 40320 - square * (1.0 / 3628800))))
    )
    odd = (quadrant & 1) == 1
    sign = (1 - (quadrant & 2)).astype(F32)
    return jnp.where(odd, -sine, cosine) * sign, jnp.where(odd, cosine, sine) * sign


def pick(value, lanes):
    return jnp.take_along_axis(value, lanes, axis=1)


def swap(value):
    return pltpu.roll(value, NF, 1)


def kernel(
    times_in,
    sites_in,
    matrix_in,
    bare_in,
    shift_in,
    transfers_in,
    out,
    inverse,
    times,
    sites,
    matrix,
    bare,
    shift,
    transfers,
    factor,
    base,
    partial,
    column,
    projected,
    table,
    outer_re,
    outer_im,
    chosen,
    send_a,
    recv_a,
    held,
    green,
    send_d,
    send_t,
    recv_d,
    recv_t,
    direct_re,
    direct_im,
    turned_re,
    turned_im,
    total,
    send_o,
    sem_in,
    sem_sa,
    sem_ra,
    sem_sd,
    sem_rd,
    sem_st,
    sem_rt,
    sem_so,
    sem_ro,
):
    w = lax.axis_index("walk")
    b = lax.axis_index("blk")
    source = (b - w) & (ND - 1)
    alone = source == w

    def along_walk(i):
        z = (w >> 1) + (4, 3, 5, 2, 6, 1, 7, 0)[i // 2]
        return ((z & 7) << 1) + ((w + i + 1) & 1)

    def along_blk(i):
        y = (b >> 1) + (2, 1, 3, 0)[i // 4]
        x = (b >> 3) + 1 - (i % 4) // 2
        return ((x & 1) << 3) + ((y & 3) << 1) + ((b + i + 1) & 1)

    barrier = pltpu.get_barrier_semaphore()

    incoming = [
        pltpu.make_async_copy(held, here, sem_in.at[k])
        for k, (held, here) in enumerate(
            (
                (times_in, times),
                (sites_in, sites),
                (matrix_in, matrix),
                (bare_in, bare),
                (shift_in, shift),
                (transfers_in, transfers),
            )
        )
    ]
    for copy in incoming:
        copy.start()
    for i in range(ND - 1):
        pl.semaphore_signal(barrier, inc=1, device_id=(along_walk(i), b), device_id_type=MESH)
        pl.semaphore_signal(barrier, inc=1, device_id=(w, along_blk(i)), device_id_type=MESH)
    for copy in incoming:
        copy.wait()

    step = lax.broadcasted_iota(jnp.int32, (16, NV), 0)
    step = jnp.where(step < 8, 64 * step, 8 * (step - 8) + 4 * (1 - NF))
    cosine, sine = sincos((step * times[...]) & (TURN - 1))
    factor[0] = cosine
    factor[1] = sine
    fine_cos = factor[0, 8:16, :]
    fine_sin = factor[1, 8:16, :]
    for g in range(0, 8, 2):
        coarse = [(factor[0, g + k : g + k + 1, :], factor[1, g + k : g + k + 1, :]) for k in range(2)]
        base[8 * g : 8 * g + 16, :] = jnp.concatenate(
            [c * fine_cos - n * fine_sin for c, n in coarse], axis=0
        ).astype(BF16)
        base[NF + 8 * g : NF + 8 * g + 16, :] = jnp.concatenate(
            [n * fine_cos + c * fine_sin for c, n in coarse], axis=0
        ).astype(BF16)

    left = lax.broadcasted_iota(jnp.int32, (NF, PACK), 1) < NF
    row_of = lax.broadcasted_iota(jnp.int32, (NF, PACK), 0)
    whole_lane = lax.broadcasted_iota(jnp.int32, (NF, PACK), 1)
    lane_of = whole_lane & (NF - 1)
    skew = (whole_lane & NF) | ((whole_lane + row_of) & (NF - 1))
    straight = (whole_lane & NF) | ((whole_lane - row_of) & (NF - 1))
    minus_left = jnp.where(left, -1.0, 1.0)
    scale = NV ** (-0.5)

    def quarter(block):
        return -minus_left * swap(block)

    def turns(blocks):
        even, odd = blocks[0] + blocks[2], blocks[1] + blocks[3]
        apart, turned = blocks[0] - blocks[2], quarter(blocks[1] - blocks[3])
        return even + odd, apart + turned, even - odd, apart - turned

    for m in range(NM):
        piece_re = bare[0:1, m * NF : m * NF + NF] * scale
        piece_im = bare[1:2, m * NF : m * NF + NF] * scale
        column[m, 0:1, :] = jnp.concatenate([piece_re, -piece_re], axis=1)
        column[m, 1:2, :] = jnp.concatenate([piece_im, piece_im], axis=1)

    for x in range(SIDE):
        rows = []
        for y in range(SIDE):
            here = jnp.where(sites[...] == SIDE * x + y, 1.0, 0.0)
            rows.append(matrix[0] * jnp.broadcast_to(here, (NF, NV)).astype(BF16))
        block = lax.dot_general(
            jnp.concatenate(rows, axis=0), base[...], (((1,), (1,)), ((), ())), preferred_element_type=F32
        )
        for y, value in enumerate(turns([block[NF * y : NF * y + NF] for y in range(SIDE)])):
            partial[SIDE * x + y] = value
    def join(y, carry):
        for x, value in enumerate(turns([partial[SIDE * x + y] for x in range(SIDE)])):
            factors = column[SIDE * x + y]
            projected[SIDE * x + y] = (value * factors[0:1] + swap(value) * factors[1:2]).astype(BF16)
        return carry

    lax.fori_loop(0, SIDE, join, 0)
    for i in range(ND):
        send_a[i] = projected[shift[along_walk(i)]]

    pl.semaphore_wait(barrier, 2 * ND - 2)

    def rows_from(peer):
        return recv_a.at[pl.ds(pl.multiple_of(peer * NF, NF), NF)]

    def copy_a(i):
        peer = along_walk(i)
        return pltpu.make_async_remote_copy(
            src_ref=send_a.at[i],
            dst_ref=rows_from(w),
            send_sem=sem_sa.at[i],
            recv_sem=sem_ra.at[w],
            device_id=(peer, b),
            device_id_type=MESH,
        )

    for i in range(ND - 1):
        copy_a(i).start()
    recv_a[pl.ds(pl.multiple_of(w * NF, NF), NF), :] = send_a[ND - 1]

    def rotate(m, carry):
        turn = ((m >> 2) * (sites[...] >> 2) + (m & 3) * (sites[...] & 3)) & 3
        sign = (1 - (turn & 2)).astype(F32)
        odd = (turn & 1).astype(F32)
        along = jnp.broadcast_to((1.0 - odd) * sign, (NF, NV)).astype(BF16)
        across = jnp.broadcast_to(odd * sign, (NF, NV)).astype(BF16)
        cosine = base[0:NF]
        sine = base[NF:PACK]
        table[m, :, 0:NV] = cosine * along + sine * across
        table[m, :, NV : 2 * NV] = sine * along - cosine * across
        return carry

    lax.fori_loop(0, NM, rotate, 0)

    for part, target in ((0, outer_re), (1, outer_im)):
        for tile in range(NV // 128):
            row = jnp.broadcast_to(bare[part : part + 1, tile * 128 : tile * 128 + 128], (128, 128))
            column = row.T
            if part == 1:
                column = jnp.where(lax.broadcasted_iota(jnp.int32, (128, 128), 1) < NF, -column, column)
            target[tile * 128 : tile * 128 + 128, :] = column

    for m in range(NM):
        position = jnp.int32(0)
        for i in range(1, NM):
            position = jnp.where(shift[i] == m, i, position)
        inverse[m] = position

    for target in (turned_re, turned_im):
        for pair in range(NM // 2):
            target[pair, 0:16, :] = jnp.zeros((16, 128), F32)
            target[pair, 80:96, :] = jnp.zeros((16, 128), F32)

    mine = shift[w]
    for i in range(ND):
        chosen[i] = shift[shift[(along_blk(i) - w) & (ND - 1)]]

    for i in range(ND - 1):
        peer = along_walk(i)
        pltpu.make_async_copy(send_a.at[i], rows_from(peer), sem_ra.at[peer]).wait()
        copy_a(i).wait_send()
    whole = recv_a[0:NV, :].astype(F32)
    sign = jnp.where(lax.broadcasted_iota(jnp.int32, (1, PACK), 1) < NF, -1.0, 1.0)
    recv_a[NV : 2 * NV, :] = (swap(whole) * sign).astype(BF16)

    def copy_d(m):
        return pltpu.make_async_remote_copy(
            src_ref=send_d.at[m],
            dst_ref=recv_d.at[b],
            send_sem=sem_sd.at[m],
            recv_sem=sem_rd.at[b],
            device_id=(m, (w + m) & (ND - 1)),
            device_id_type=MESH,
        )

    def own_d(m):
        return pltpu.make_async_copy(send_d.at[m], recv_d.at[b], sem_rd.at[b])

    def is_own(m):
        return jnp.logical_and(alone, m == w)

    diagonal = jnp.where(jnp.logical_and(left, row_of == lane_of), 1.0, 0.0)

    def assemble(group):
        raw = held.at[group % 2]
        for k in range(4):
            m = 4 * group + k
            part = raw[k * NF : (k + 1) * NF, :] + diagonal * (mine == m).astype(F32)
            rows = slice(m * NF, m * NF + NF)
            value = outer_re[rows, :] * part + outer_im[rows, :] * swap(part)
            green[m] = value.astype(BF16)
            send_d[m] = pick(value, skew).astype(BF16)

    for group in range(NM // 4 + 1):
        if group < NM // 4:
            held[group % 2] = jnp.dot(
                table[4 * group : 4 * group + 4].reshape(4 * NF, 2 * NV), recv_a[...], preferred_element_type=F32
            )
        if group > 0:
            assemble(group - 1)
            for k in range(4):
                m = 4 * (group - 1) + k

                @pl.when(jnp.logical_not(is_own(m)))
                def _():
                    copy_d(m).start()

    @pl.when(alone)
    def _():
        own_d(w).start()

    def copy_t(i):
        return pltpu.make_async_remote_copy(
            src_ref=send_t.at[i],
            dst_ref=recv_t.at[b],
            send_sem=sem_st.at[i],
            recv_sem=sem_rt.at[b],
            device_id=(w, along_blk(i)),
            device_id_type=MESH,
        )

    for i in range(ND - 1):
        send_t[i] = green[chosen[i]]
        copy_t(i).start()
    recv_t[b] = green[chosen[ND - 1]]

    def arrive_b(u, carry):
        pltpu.make_async_copy(green.at[0], recv_d.at[u], sem_rd.at[u]).wait()

        @pl.when(u != b)
        def _():
            pltpu.make_async_copy(green.at[0], recv_t.at[u], sem_rt.at[u]).wait()

        return carry

    def pair_up(step, carry):
        for u in range(16):
            arrive_b(16 * step + u, 0)
        for k in range(8):
            pair = 8 * step + k
            even = recv_d[2 * pair].astype(F32)
            other = recv_d[2 * pair + 1].astype(F32)
            direct_re[pair] = jnp.where(left, even, swap(other))
            direct_im[pair] = jnp.where(left, swap(even), other)
            both = recv_t[pl.ds(2 * pair, 2)].astype(F32).reshape(2 * NF, PACK).T
            turned_re[pair, 16 : 16 + NF, :] = pick(both[0:NF], skew)
            turned_im[pair, 16 : 16 + NF, :] = pick(both[NF:PACK], skew)
        return carry

    lax.fori_loop(0, NM // 16, pair_up, 0)

    def peer_o(i):
        step = i >> 2
        y = (b >> 1) + 2 - step + 3 * (step >> 1) - 2 * (step & (step >> 1))
        x = (b >> 3) + 1 - ((i & 3) >> 1)
        return ((x & 1) << 3) + ((y & 3) << 1) + ((b + i + 1) & 1)

    def copy_o(i):
        return pltpu.make_async_remote_copy(
            src_ref=send_o.at[i],
            dst_ref=out.at[source],
            send_sem=sem_so.at[i],
            recv_sem=sem_ro.at[source],
            device_id=(w, peer_o(i)),
            device_id_type=MESH,
        )

    def window(i, carry):
        peer = peer_o(i)
        offsets = [transfers[2 * peer + k] for k in range(2)]

        def multiply(step, carry):
            first = pl.multiple_of(step * BAND, BAND)
            band = pl.ds(first, BAND)
            sums = [[jnp.zeros((BAND, PACK), F32)] * 2 for k in range(2)]
            for pair in range(NM // 2):
                near_re = direct_re[pair, band]
                near_im = direct_im[pair, band]
                for k in range(2):
                    far_re = turned_re[pair, pl.ds(offsets[k] + first, BAND), :]
                    far_im = turned_im[pair, pl.ds(offsets[k] + first, BAND), :]
                    sums[k] = [
                        sums[k][0] + (near_re * far_re - near_im * far_im),
                        sums[k][1] + (near_re * far_im + near_im * far_re),
                    ]
            for k in range(2):
                total[2 * k, band] = sums[k][0]
                total[2 * k + 1, band] = sums[k][1]
            return carry

        lax.fori_loop(0, NF // BAND, multiply, 0)
        for k in range(2):
            sum_re, sum_im = [value + swap(value) for value in (total[2 * k], total[2 * k + 1])]
            nu = offsets[k] - NQ // 2
            row = row_of + nu
            col = lane_of + nu
            keep = (row >= 0) & (row < NF) & (col >= 0) & (col < NF)
            result = pick(jnp.where(left, sum_re, sum_im), straight)
            send_o[i, k] = jnp.where(keep, result, 0.0).astype(BF16)

        @pl.when(i < ND - 1)
        def _():
            copy_o(i).start()

        return carry

    lax.fori_loop(0, ND, window, 0)
    own_o = pltpu.make_async_copy(send_o.at[ND - 1], out.at[source], sem_ro.at[source])
    own_o.start()

    def arrive_o(i, carry):
        pltpu.make_async_copy(send_o.at[i], out.at[i], sem_ro.at[i]).wait()
        return carry

    lax.fori_loop(0, ND, arrive_o, 0)

    for i in range(ND - 1):
        copy_t(i).wait_send()
        copy_o(i).wait_send()

    def drain_d(m, carry):
        @pl.when(jnp.logical_not(is_own(m)))
        def _():
            copy_d(m).wait_send()

        return carry

    lax.fori_loop(0, NM, drain_d, 0)


def spread_out(inverse, blocks, out):
    left = lax.broadcasted_iota(jnp.int32, (NF, PACK), 1) < NF
    for tile in range(NM // 2):
        even = blocks[inverse[2 * tile]].astype(F32)
        other = blocks[inverse[2 * tile + 1]].astype(F32)
        for k in range(2):
            out[0, k, :, tile * 128 : tile * 128 + 128] = jnp.where(left, even[k], swap(other[k]))
            out[1, k, :, tile * 128 : tile * 128 + 128] = jnp.where(left, swap(even[k]), other[k])


def shards(vertex_times, vertex_sites, vertex_matrix, bare_green, transfer_momentum, transfers):
    vmem = pl.BlockSpec(memory_space=pltpu.VMEM)
    smem = pl.BlockSpec(memory_space=pltpu.SMEM)
    here = pl.BlockSpec(memory_space=pl.ANY)
    sems = pltpu.SemaphoreType.DMA((ND,))
    blocks = pltpu.VMEM((ND, NF, PACK), BF16)
    pairs = pltpu.VMEM((NM // 2, NF, PACK), F32)
    padded = pltpu.VMEM((NM // 2, NF + 32, PACK), F32)
    results, inverse = pl.pallas_call(
        kernel,
        out_shape=[
            jax.ShapeDtypeStruct((ND, 2, NF, PACK), BF16),
            jax.ShapeDtypeStruct((NM,), jnp.int32),
        ],
        in_specs=[pl.BlockSpec(memory_space=pltpu.HBM)] * 6,
        out_specs=[here, smem],
        scratch_shapes=[
            pltpu.VMEM((1, NV), jnp.int32),
            pltpu.VMEM((1, NV), jnp.int32),
            pltpu.VMEM((1, NF, NV), BF16),
            pltpu.VMEM((2, NV), F32),
            pltpu.SMEM((NM,), jnp.int32),
            pltpu.SMEM((NQ,), jnp.int32),
            pltpu.VMEM((2, 16, NV), F32),
            pltpu.VMEM((PACK, NV), BF16),
            pltpu.VMEM((NM, NF, PACK), F32),
            pltpu.VMEM((NM, 8, PACK), F32),
            blocks,
            pltpu.VMEM((NM, NF, 2 * NV), BF16),
            pltpu.VMEM((NV, PACK), F32),
            pltpu.VMEM((NV, PACK), F32),
            pltpu.SMEM((NM,), jnp.int32),
            blocks,
            pltpu.VMEM((2 * NV, PACK), BF16),
            pltpu.VMEM((2, 4 * NF, PACK), F32),
            blocks,
            blocks,
            blocks,
            blocks,
            blocks,
            pairs,
            pairs,
            padded,
            padded,
            pltpu.VMEM((4, NF, PACK), F32),
            pltpu.VMEM((ND, 2, NF, PACK), BF16),
            pltpu.SemaphoreType.DMA((6,)),
        ]
        + [sems] * 8,
        compiler_params=pltpu.CompilerParams(collective_id=0, has_side_effects=True, vmem_limit_bytes=24 * 2**20),
    )(*[pltpu.with_memory_space_constraint(a, pltpu.HBM) for a in (vertex_times, vertex_sites, vertex_matrix, bare_green, transfer_momentum, transfers)])
    return pl.pallas_call(
        spread_out,
        out_shape=jax.ShapeDtypeStruct((2, 2, NF, NV), F32),
        in_specs=[smem, vmem],
        out_specs=vmem,
        compiler_params=pltpu.CompilerParams(vmem_limit_bytes=16 * 2**20),
    )(inverse, results)


def solution(mesh):
    return jax.shard_map(
        shards,
        mesh=mesh,
        in_specs=(P("blk", None), P("blk", None), P("blk", "walk", None), P(), P(), P()),
        out_specs=P(None, "blk", "walk", None),
        check_vma=False,
    )
```

```python
import math

import jax
import jax.numpy as jnp
from jax import lax
from jax.experimental import pallas as pl
from jax.experimental.pallas import tpu as pltpu
from jax.sharding import PartitionSpec as P

NM = 16
NF = 64
NV = 1024
NT = 4096
NQ = 32
SIDE = 4
ND = 16
PACK = 2 * NF
TURN = 8 * NT
QUARTER = TURN // 4
BAND = 16
MESH = pl.DeviceIdType.MESH
F32 = jnp.float32
BF16 = jnp.bfloat16


def sincos(phase):
    quadrant = (phase + QUARTER // 2) >> 13
    angle = (phase - (quadrant << 13)).astype(F32) * (2.0 * math.pi / TURN)
    square = angle * angle
    sine = angle * (
        1.0 + square * (-1.0 / 6 + square * (1.0 / 120 + square * (-1.0 / 5040 + square * (1.0 / 362880))))
    )
    cosine = 1.0 + square * (
        -0.5 + square * (1.0 / 24 + square * (-1.0 / 720 + square * (1.0 / 40320 - square * (1.0 / 3628800))))
    )
    odd = (quadrant & 1) == 1
    sign = (1 - (quadrant & 2)).astype(F32)
    return jnp.where(odd, -sine, cosine) * sign, jnp.where(odd, cosine, sine) * sign


def pick(value, lanes):
    return jnp.take_along_axis(value, lanes, axis=1)


def swap(value):
    return pltpu.roll(value, NF, 1)


def kernel(
    times_in,
    sites_in,
    matrix_in,
    bare_in,
    shift_in,
    transfers_in,
    out,
    inverse,
    times,
    sites,
    matrix,
    bare,
    shift,
    transfers,
    factor,
    base,
    partial,
    column,
    projected,
    table,
    outer_re,
    outer_im,
    chosen,
    send_a,
    recv_a,
    held,
    green,
    send_d,
    send_t,
    recv_d,
    recv_t,
    direct_re,
    direct_im,
    turned_re,
    turned_im,
    total,
    send_o,
    sem_in,
    sem_sa,
    sem_ra,
    sem_sd,
    sem_rd,
    sem_st,
    sem_rt,
    sem_so,
    sem_ro,
):
    w = lax.axis_index("walk")
    b = lax.axis_index("blk")
    source = (b - w) & (ND - 1)
    alone = source == w

    def along_walk(i):
        z = (w >> 1) + (4, 3, 5, 2, 6, 1, 7, 0)[i // 2]
        return ((z & 7) << 1) + ((w + i + 1) & 1)

    def along_blk(i):
        y = (b >> 1) + (2, 1, 3, 0)[i // 4]
        x = (b >> 3) + 1 - (i % 4) // 2
        return ((x & 1) << 3) + ((y & 3) << 1) + ((b + i + 1) & 1)

    barrier = pltpu.get_barrier_semaphore()

    incoming = [
        pltpu.make_async_copy(held, here, sem_in.at[k])
        for k, (held, here) in enumerate(
            (
                (times_in, times),
                (sites_in, sites),
                (matrix_in, matrix),
                (bare_in, bare),
                (shift_in, shift),
                (transfers_in, transfers),
            )
        )
    ]
    for copy in incoming:
        copy.start()
    for i in range(ND - 1):
        pl.semaphore_signal(barrier, inc=1, device_id=(along_walk(i), b), device_id_type=MESH)
        pl.semaphore_signal(barrier, inc=1, device_id=(w, along_blk(i)), device_id_type=MESH)
    for copy in incoming:
        copy.wait()

    step = lax.broadcasted_iota(jnp.int32, (16, NV), 0)
    step = jnp.where(step < 8, 64 * step, 8 * (step - 8) + 4 * (1 - NF))
    cosine, sine = sincos((step * times[...]) & (TURN - 1))
    factor[0] = cosine
    factor[1] = sine
    fine_cos = factor[0, 8:16, :]
    fine_sin = factor[1, 8:16, :]
    for g in range(0, 8, 2):
        coarse = [(factor[0, g + k : g + k + 1, :], factor[1, g + k : g + k + 1, :]) for k in range(2)]
        base[8 * g : 8 * g + 16, :] = jnp.concatenate(
            [c * fine_cos - n * fine_sin for c, n in coarse], axis=0
        ).astype(BF16)
        base[NF + 8 * g : NF + 8 * g + 16, :] = jnp.concatenate(
            [n * fine_cos + c * fine_sin for c, n in coarse], axis=0
        ).astype(BF16)

    left = lax.broadcasted_iota(jnp.int32, (NF, PACK), 1) < NF
    row_of = lax.broadcasted_iota(jnp.int32, (NF, PACK), 0)
    whole_lane = lax.broadcasted_iota(jnp.int32, (NF, PACK), 1)
    lane_of = whole_lane & (NF - 1)
    skew = (whole_lane & NF) | ((whole_lane + row_of) & (NF - 1))
    straight = (whole_lane & NF) | ((whole_lane - row_of) & (NF - 1))
    minus_left = jnp.where(left, -1.0, 1.0)
    scale = NV ** (-0.5)

    def quarter(block):
        return -minus_left * swap(block)

    def turns(blocks):
        even, odd = blocks[0] + blocks[2], blocks[1] + blocks[3]
        apart, turned = blocks[0] - blocks[2], quarter(blocks[1] - blocks[3])
        return even + odd, apart + turned, even - odd, apart - turned

    for m in range(NM):
        piece_re = bare[0:1, m * NF : m * NF + NF] * scale
        piece_im = bare[1:2, m * NF : m * NF + NF] * scale
        column[m, 0:1, :] = jnp.concatenate([piece_re, -piece_re], axis=1)
        column[m, 1:2, :] = jnp.concatenate([piece_im, piece_im], axis=1)

    for x in range(SIDE):
        rows = []
        for y in range(SIDE):
            here = jnp.where(sites[...] == SIDE * x + y, 1.0, 0.0)
            rows.append(matrix[0] * jnp.broadcast_to(here, (NF, NV)).astype(BF16))
        block = lax.dot_general(
            jnp.concatenate(rows, axis=0), base[...], (((1,), (1,)), ((), ())), preferred_element_type=F32
        )
        for y, value in enumerate(turns([block[NF * y : NF * y + NF] for y in range(SIDE)])):
            partial[SIDE * x + y] = value
    def join(y, carry):
        for x, value in enumerate(turns([partial[SIDE * x + y] for x in range(SIDE)])):
            factors = column[SIDE * x + y]
            projected[SIDE * x + y] = (value * factors[0:1] + swap(value) * factors[1:2]).astype(BF16)
        return carry

    lax.fori_loop(0, SIDE, join, 0)
    for i in range(ND):
        send_a[i] = projected[shift[along_walk(i)]]

    pl.semaphore_wait(barrier, 2 * ND - 2)

    def rows_from(peer):
        return recv_a.at[pl.ds(pl.multiple_of(peer * NF, NF), NF)]

    def copy_a(i):
        peer = along_walk(i)
        return pltpu.make_async_remote_copy(
            src_ref=send_a.at[i],
            dst_ref=rows_from(w),
            send_sem=sem_sa.at[i],
            recv_sem=sem_ra.at[w],
            device_id=(peer, b),
            device_id_type=MESH,
        )

    for i in range(ND - 1):
        copy_a(i).start()
    recv_a[pl.ds(pl.multiple_of(w * NF, NF), NF), :] = send_a[ND - 1]

    def rotate(m, carry):
        turn = ((m >> 2) * (sites[...] >> 2) + (m & 3) * (sites[...] & 3)) & 3
        sign = (1 - (turn & 2)).astype(F32)
        odd = (turn & 1).astype(F32)
        along = jnp.broadcast_to((1.0 - odd) * sign, (NF, NV)).astype(BF16)
        across = jnp.broadcast_to(odd * sign, (NF, NV)).astype(BF16)
        cosine = base[0:NF]
        sine = base[NF:PACK]
        table[m, :, 0:NV] = cosine * along + sine * across
        table[m, :, NV : 2 * NV] = sine * along - cosine * across
        return carry

    lax.fori_loop(0, NM, rotate, 0)

    for part, target in ((0, outer_re), (1, outer_im)):
        for tile in range(NV // 128):
            row = jnp.broadcast_to(bare[part : part + 1, tile * 128 : tile * 128 + 128], (128, 128))
            column = row.T
            if part == 1:
                column = jnp.where(lax.broadcasted_iota(jnp.int32, (128, 128), 1) < NF, -column, column)
            target[tile * 128 : tile * 128 + 128, :] = column

    for m in range(NM):
        position = jnp.int32(0)
        for i in range(1, NM):
            position = jnp.where(shift[i] == m, i, position)
        inverse[m] = position

    for target in (turned_re, turned_im):
        for pair in range(NM // 2):
            target[pair, 0:16, :] = jnp.zeros((16, 128), F32)
            target[pair, 80:96, :] = jnp.zeros((16, 128), F32)

    mine = shift[w]
    for i in range(ND):
        chosen[i] = shift[shift[(along_blk(i) - w) & (ND - 1)]]

    for i in range(ND - 1):
        peer = along_walk(i)
        pltpu.make_async_copy(send_a.at[i], rows_from(peer), sem_ra.at[peer]).wait()
        copy_a(i).wait_send()
    whole = recv_a[0:NV, :].astype(F32)
    sign = jnp.where(lax.broadcasted_iota(jnp.int32, (1, PACK), 1) < NF, -1.0, 1.0)
    recv_a[NV : 2 * NV, :] = (swap(whole) * sign).astype(BF16)

    def copy_d(m):
        return pltpu.make_async_remote_copy(
            src_ref=send_d.at[m],
            dst_ref=recv_d.at[b],
            send_sem=sem_sd.at[m],
            recv_sem=sem_rd.at[b],
            device_id=(m, (w + m) & (ND - 1)),
            device_id_type=MESH,
        )

    def own_d(m):
        return pltpu.make_async_copy(send_d.at[m], recv_d.at[b], sem_rd.at[b])

    def is_own(m):
        return jnp.logical_and(alone, m == w)

    diagonal = jnp.where(jnp.logical_and(left, row_of == lane_of), 1.0, 0.0)

    def assemble(group):
        raw = held.at[group % 2]
        for k in range(4):
            m = 4 * group + k
            part = raw[k * NF : (k + 1) * NF, :] + diagonal * (mine == m).astype(F32)
            rows = slice(m * NF, m * NF + NF)
            value = outer_re[rows, :] * part + outer_im[rows, :] * swap(part)
            green[m] = value.astype(BF16)
            send_d[m] = pick(value, skew).astype(BF16)

    for group in range(NM // 4 + 1):
        if group < NM // 4:
            held[group % 2] = jnp.dot(
                table[4 * group : 4 * group + 4].reshape(4 * NF, 2 * NV), recv_a[...], preferred_element_type=F32
            )
        if group > 0:
            assemble(group - 1)
            for k in range(4):
                m = 4 * (group - 1) + k

                @pl.when(jnp.logical_not(is_own(m)))
                def _():
                    copy_d(m).start()

    @pl.when(alone)
    def _():
        own_d(w).start()

    def copy_t(i):
        return pltpu.make_async_remote_copy(
            src_ref=send_t.at[i],
            dst_ref=recv_t.at[b],
            send_sem=sem_st.at[i],
            recv_sem=sem_rt.at[b],
            device_id=(w, along_blk(i)),
            device_id_type=MESH,
        )

    for i in range(ND - 1):
        send_t[i] = green[chosen[i]]
        copy_t(i).start()
    recv_t[b] = green[chosen[ND - 1]]

    def arrive_b(u, carry):
        pltpu.make_async_copy(green.at[0], recv_d.at[u], sem_rd.at[u]).wait()

        @pl.when(u != b)
        def _():
            pltpu.make_async_copy(green.at[0], recv_t.at[u], sem_rt.at[u]).wait()

        return carry

    def pair_up(step, carry):
        for u in range(16):
            arrive_b(16 * step + u, 0)
        for k in range(8):
            pair = 8 * step + k
            even = recv_d[2 * pair].astype(F32)
            other = recv_d[2 * pair + 1].astype(F32)
            direct_re[pair] = jnp.where(left, even, swap(other))
            direct_im[pair] = jnp.where(left, swap(even), other)
            both = recv_t[pl.ds(2 * pair, 2)].astype(F32).reshape(2 * NF, PACK).T
            turned_re[pair, 16 : 16 + NF, :] = pick(both[0:NF], skew)
            turned_im[pair, 16 : 16 + NF, :] = pick(both[NF:PACK], skew)
        return carry

    lax.fori_loop(0, NM // 16, pair_up, 0)

    def peer_o(i):
        up = jnp.where(i < 4, 2, jnp.where(i < 12, 1 + 2 * (i & 1), 0))
        q = jnp.where(jnp.logical_and(i >= 4, i < 12), (i - 4) >> 1, i & 3)
        y = (b >> 1) + up
        x = (b >> 3) + 1 - (q >> 1)
        return ((x & 1) << 3) + ((y & 3) << 1) + ((b + q + 1) & 1)

    def copy_o(i):
        return pltpu.make_async_remote_copy(
            src_ref=send_o.at[i],
            dst_ref=out.at[source],
            send_sem=sem_so.at[i],
            recv_sem=sem_ro.at[source],
            device_id=(w, peer_o(i)),
            device_id_type=MESH,
        )

    def window(i, carry):
        peer = peer_o(i)
        offsets = [transfers[2 * peer + k] for k in range(2)]

        def multiply(step, carry):
            first = pl.multiple_of(step * BAND, BAND)
            band = pl.ds(first, BAND)
            sums = [[jnp.zeros((BAND, PACK), F32)] * 2 for k in range(2)]
            for pair in range(NM // 2):
                near_re = direct_re[pair, band]
                near_im = direct_im[pair, band]
                for k in range(2):
                    far_re = turned_re[pair, pl.ds(offsets[k] + first, BAND), :]
                    far_im = turned_im[pair, pl.ds(offsets[k] + first, BAND), :]
                    sums[k] = [
                        sums[k][0] + (near_re * far_re - near_im * far_im),
                        sums[k][1] + (near_re * far_im + near_im * far_re),
                    ]
            for k in range(2):
                total[2 * k, band] = sums[k][0]
                total[2 * k + 1, band] = sums[k][1]
            return carry

        lax.fori_loop(0, NF // BAND, multiply, 0)
        for k in range(2):
            sum_re, sum_im = [value + swap(value) for value in (total[2 * k], total[2 * k + 1])]
            nu = offsets[k] - NQ // 2
            row = row_of + nu
            col = lane_of + nu
            keep = (row >= 0) & (row < NF) & (col >= 0) & (col < NF)
            result = pick(jnp.where(left, sum_re, sum_im), straight)
            send_o[i, k] = jnp.where(keep, result, 0.0).astype(BF16)

        @pl.when(i < ND - 1)
        def _():
            copy_o(i).start()

        return carry

    lax.fori_loop(0, ND, window, 0)
    own_o = pltpu.make_async_copy(send_o.at[ND - 1], out.at[source], sem_ro.at[source])
    own_o.start()

    def arrive_o(i, carry):
        pltpu.make_async_copy(send_o.at[i], out.at[i], sem_ro.at[i]).wait()
        return carry

    lax.fori_loop(0, ND, arrive_o, 0)

    for i in range(ND - 1):
        copy_t(i).wait_send()
        copy_o(i).wait_send()

    def drain_d(m, carry):
        @pl.when(jnp.logical_not(is_own(m)))
        def _():
            copy_d(m).wait_send()

        return carry

    lax.fori_loop(0, NM, drain_d, 0)


def spread_out(inverse, blocks, out):
    left = lax.broadcasted_iota(jnp.int32, (NF, PACK), 1) < NF
    for tile in range(NM // 2):
        even = blocks[inverse[2 * tile]].astype(F32)
        other = blocks[inverse[2 * tile + 1]].astype(F32)
        for k in range(2):
            out[0, k, :, tile * 128 : tile * 128 + 128] = jnp.where(left, even[k], swap(other[k]))
            out[1, k, :, tile * 128 : tile * 128 + 128] = jnp.where(left, swap(even[k]), other[k])


def shards(vertex_times, vertex_sites, vertex_matrix, bare_green, transfer_momentum, transfers):
    vmem = pl.BlockSpec(memory_space=pltpu.VMEM)
    smem = pl.BlockSpec(memory_space=pltpu.SMEM)
    here = pl.BlockSpec(memory_space=pl.ANY)
    sems = pltpu.SemaphoreType.DMA((ND,))
    blocks = pltpu.VMEM((ND, NF, PACK), BF16)
    pairs = pltpu.VMEM((NM // 2, NF, PACK), F32)
    padded = pltpu.VMEM((NM // 2, NF + 32, PACK), F32)
    results, inverse = pl.pallas_call(
        kernel,
        out_shape=[
            jax.ShapeDtypeStruct((ND, 2, NF, PACK), BF16),
            jax.ShapeDtypeStruct((NM,), jnp.int32),
        ],
        in_specs=[pl.BlockSpec(memory_space=pltpu.HBM)] * 6,
        out_specs=[here, smem],
        scratch_shapes=[
            pltpu.VMEM((1, NV), jnp.int32),
            pltpu.VMEM((1, NV), jnp.int32),
            pltpu.VMEM((1, NF, NV), BF16),
            pltpu.VMEM((2, NV), F32),
            pltpu.SMEM((NM,), jnp.int32),
            pltpu.SMEM((NQ,), jnp.int32),
            pltpu.VMEM((2, 16, NV), F32),
            pltpu.VMEM((PACK, NV), BF16),
            pltpu.VMEM((NM, NF, PACK), F32),
            pltpu.VMEM((NM, 8, PACK), F32),
            blocks,
            pltpu.VMEM((NM, NF, 2 * NV), BF16),
            pltpu.VMEM((NV, PACK), F32),
            pltpu.VMEM((NV, PACK), F32),
            pltpu.SMEM((NM,), jnp.int32),
            blocks,
            pltpu.VMEM((2 * NV, PACK), BF16),
            pltpu.VMEM((2, 4 * NF, PACK), F32),
            blocks,
            blocks,
            blocks,
            blocks,
            blocks,
            pairs,
            pairs,
            padded,
            padded,
            pltpu.VMEM((4, NF, PACK), F32),
            pltpu.VMEM((ND, 2, NF, PACK), BF16),
            pltpu.SemaphoreType.DMA((6,)),
        ]
        + [sems] * 8,
        compiler_params=pltpu.CompilerParams(collective_id=0, has_side_effects=True, vmem_limit_bytes=24 * 2**20),
    )(*[pltpu.with_memory_space_constraint(a, pltpu.HBM) for a in (vertex_times, vertex_sites, vertex_matrix, bare_green, transfer_momentum, transfers)])
    return pl.pallas_call(
        spread_out,
        out_shape=jax.ShapeDtypeStruct((2, 2, NF, NV), F32),
        in_specs=[smem, vmem],
        out_specs=vmem,
        compiler_params=pltpu.CompilerParams(vmem_limit_bytes=16 * 2**20),
    )(inverse, results)


def solution(mesh):
    return jax.shard_map(
        shards,
        mesh=mesh,
        in_specs=(P("blk", None), P("blk", None), P("blk", "walk", None), P(), P(), P()),
        out_specs=P(None, "blk", "walk", None),
        check_vma=False,
    )
```
